32 devices in a mesh: blk: 8 (over z, x), team: 4 (over y, core).
Axes of the slice: x: 2, y: 2, z: 4, core: 2. Of those that a mesh axis runs over, the one named last changes fastest.
Arguments:
- points: float32 [2048, 1024], P('blk'), may hold values from -80 to 80
- probes: float32 [2048, 256], P('blk'), may hold values from -6 to 6
Outputs:
- product: float32 [2048, 256], P(('blk', 'team'))
The draws below stay inside these ranges and needn't reach their ends.
All inputs are finite; a program needn't handle non-finite values.
Results may differ from the reference program's by a relative error of at most 0.00014.
Values sent between devices are 32-bit elements; how exact they have to be, the bound alone decides.
A program may use at most 64 MiB of HBM per device.

```python
import jax
import jax.numpy as jnp
from jax import lax

D = 1024
R = 256
LATENT = 16
ROWS = 256
POINTS = 2048
N_BLK = 8


def draw_points(key, part):
    first = jax.random.fold_in(key, 11)
    second = jax.random.fold_in(key, 23)
    third = jax.random.fold_in(key, 37)
    latent = jnp.clip(jax.random.normal(first, (POINTS, LATENT), jnp.float32), -4.0, 4.0)
    mixing = jnp.clip(jax.random.normal(second, (LATENT, D), jnp.float32), -4.0, 4.0) / 4.0
    noise = jnp.clip(jax.random.normal(third, (POINTS, D), jnp.float32), -4.0, 4.0) * 0.3
    return jnp.dot(latent, mixing) + noise


def block_scale(own_key, dims, shards, smallest, high):
    gain, own = 1.0, jax.random.fold_in(own_key, 6)
    for axis_at, parts in shards:
        steps = jnp.exp(jax.random.uniform(jax.random.fold_in(own, axis_at), (parts,), jnp.float32, smallest / len(shards), high / len(shards)))
        gain = gain * jnp.repeat(steps, dims[axis_at] // parts).reshape([-1 if axis == axis_at else 1 for axis in range(len(dims))])
    return gain


def bell_draw(own_key, extent, spread, most, pieces=(), dtype=jnp.bfloat16):
    factor_of = block_scale(own_key, extent, pieces, -0.22, 0.18) if pieces else 1.0
    drawn = jax.random.normal(own_key, extent, jnp.float32) * spread * factor_of
    return jnp.minimum(jnp.maximum(drawn, -most), most).astype(dtype)


def setup_inputs(seed: int = 0) -> dict:
    seeds = jax.random.split(jax.random.key(seed), 3)
    points = draw_points(jax.random.fold_in(seeds[2], 71), 0)
    probes = bell_draw(seeds[1], (POINTS, R), 1.0, 6.0, ((0, 8),), jnp.float32)
    return dict(points=points, probes=probes)


def reference(points, probes):
    scale = 2.0 / points.shape[1]
    sq = jnp.sum(points * points, axis=1)
    blocks = points.reshape(N_BLK, ROWS, points.shape[1])
    sq_blocks = sq.reshape(N_BLK, ROWS)

    def one_block(pair):
        rows, rows_sq = pair
        cross = lax.dot_general(rows, points, (((1,), (1,)), ((), ())), precision=lax.Precision.HIGHEST, preferred_element_type=jnp.float32)
        arg = (rows_sq[:, None] + sq[None, :] - 2.0 * cross) * scale
        kernel = jnp.exp(-jnp.maximum(arg, 0.0))
        return jnp.dot(kernel, probes, precision=lax.Precision.HIGHEST, preferred_element_type=jnp.float32)

    result = lax.map(one_block, (blocks, sq_blocks))
    return result.reshape(N_BLK * ROWS, probes.shape[1])
```

```python
import functools

import jax
import jax.numpy as jnp
from jax import lax
from jax.experimental import pallas as pl
from jax.experimental.pallas import tpu as pltpu
from jax.sharding import PartitionSpec as P

MESH = pl.DeviceIdType.MESH


def kernel(
    outer,
    inner,
    points_hbm,
    probes_hbm,
    out_ref,
    layer_points,
    layer_probes,
    points_high,
    points_low,
    probes_high,
    probes_low,
    layer_sq,
    visitors,
    visitor_terms,
    visitor_sq,
    sums,
    returned,
    load_sem,
    visit_send,
    visit_recv,
    row_send,
    share_send,
    row_recv,
    back_send,
    back_recv,
):
    rows, width = points_hbm.shape
    piece = visitors.shape[1]
    half = rows // 2
    sub = half // 2
    scale = 2.0 / width
    block = lax.axis_index("blk")
    team = lax.axis_index("team")
    z = block // inner
    x = lax.rem(block, inner)
    core = lax.rem(team, 2)
    sibling = {"team": team + 1 - 2 * core}

    def at(layer, column):
        return {"blk": layer * inner + column}

    def inside(layer):
        return (layer >= 0) & (layer < outer)

    def remote(src, dst, send, recv, target):
        return pltpu.make_async_remote_copy(
            src_ref=src, dst_ref=dst, send_sem=send, recv_sem=recv, device_id=target, device_id_type=MESH
        )

    def wait_recv(ref, sem):
        pltpu.make_async_copy(ref, ref, sem).wait()

    own_rows = pl.ds(pl.multiple_of(team * piece, piece), piece)

    def onward(layer, way, turn, first=False):
        where = pl.ds(turn * (piece // 2), piece // 2)
        return remote(
            points_hbm.at[pl.ds(pl.multiple_of(team * piece + turn * (piece // 2), piece // 2), piece // 2)]
            if first
            else visitors.at[layer, where],
            visitors.at[layer, where],
            visit_send.at[layer, (way + 1) // 2, turn],
            visit_recv.at[layer, turn],
            at(z + way, x),
        )

    def slot(column, part, side):
        return (column * 2 + part) * 2 + side

    def slot_rows(column, part, side):
        return pl.ds(pl.multiple_of(column * rows + part * half + side * sub, sub), sub)

    def across(step, part):
        source = pl.ds(pl.multiple_of(part * half + core * sub, sub), sub)
        where = slot_rows(x, part, core)
        return [
            remote(
                src.at[source],
                dst.at[where],
                row_send.at[step - 1, part, which],
                row_recv.at[slot(x, part, core), which],
                at(z, lax.rem(x + step, inner)),
            )
            for which, (src, dst) in enumerate(((points_hbm, layer_points), (probes_hbm, layer_probes)))
        ]

    def share(step, part):
        column = lax.rem(x + step, inner)
        where = slot_rows(column, part, core)
        return [
            remote(
                ref.at[where],
                ref.at[where],
                share_send.at[step - 1, part, which],
                row_recv.at[slot(column, part, core), which],
                sibling,
            )
            for which, ref in enumerate((layer_points, layer_probes))
        ]

    def wait_rows(column, part, side):
        for which, ref in enumerate((layer_points, layer_probes)):
            wait_recv(ref.at[slot_rows(column, part, side)], row_recv.at[slot(column, part, side), which])

    def back(layer, turn):
        where = pl.ds(turn * (piece // 2), piece // 2)
        return remote(
            sums.at[layer, where],
            returned.at[z, where],
            back_send.at[layer, turn],
            back_recv.at[z, turn],
            at(layer, x),
        )

    def half_rows(column, part):
        return pl.ds(pl.multiple_of(column * rows + part * half, half), half)

    def two_terms(values):
        high = values.astype(jnp.bfloat16)
        return high, (values - high.astype(jnp.float32)).astype(jnp.bfloat16)

    def four_products(stacked, high, low, contract):
        count = stacked.shape[0] // 2
        dot = functools.partial(
            lax.dot_general,
            dimension_numbers=(contract, ((), ())),
            preferred_element_type=jnp.float32,
        )
        by_high, by_low = dot(stacked, high), dot(stacked, low)
        return by_high[:count] + (by_high[count:] + by_low[:count] + by_low[count:])

    def prepare_rows(column, part):
        where = half_rows(column, part)
        values = layer_points[where, :]
        total = jnp.sum(values * values, axis=1, keepdims=True)
        layer_sq[column * 2 + part] = jnp.broadcast_to(total, (half, 128)).T[0:1, :]
        points_high[where, :], points_low[where, :] = two_terms(values)
        probes_high[where, :], probes_low[where, :] = two_terms(layer_probes[where, :])

    def prepare_visitor(layer, begin=0, count=piece):
        values = visitors[layer, begin : begin + count, :]
        visitor_sq[layer, begin : begin + count] = jnp.sum(values * values, axis=1, keepdims=True)
        high, low = two_terms(values)
        visitor_terms[layer, begin : begin + count, :] = high
        visitor_terms[layer, piece + begin : piece + begin + count, :] = low

    def pair(layer, column, parts, fresh=False, begin=0, count=piece):
        first = parts[0]
        where = pl.ds(pl.multiple_of(column * rows + first * half, half), half * len(parts))
        cross = four_products(
            jnp.concatenate(
                [
                    visitor_terms[layer, begin : begin + count, :],
                    visitor_terms[layer, piece + begin : piece + begin + count, :],
                ],
                axis=0,
            ),
            points_high[where, :],
            points_low[where, :],
            ((1,), (1,)),
        )
        row_sq = jnp.concatenate([layer_sq[column * 2 + part] for part in parts], axis=1)
        arg = (visitor_sq[layer, begin : begin + count] + row_sq - 2.0 * cross) * scale
        value = jnp.exp(-jnp.maximum(arg, 0.0))
        product = four_products(
            jnp.concatenate(two_terms(value), axis=0),
            probes_high[where, :],
            probes_low[where, :],
            ((1,), (0,)),
        )
        kept = slice(begin, begin + count)
        sums[layer, kept, :] = product if fresh else sums[layer, kept, :] + product

    barrier = pltpu.get_barrier_semaphore()
    for way in (1, -1):
        @pl.when(inside(z + way))
        def _(way=way):
            pl.semaphore_signal(barrier, inc=1, device_id=at(z + way, x), device_id_type=MESH)
    for step in range(1, inner):
        pl.semaphore_signal(barrier, inc=1, device_id=at(z, lax.rem(x + step, inner)), device_id_type=MESH)
    pl.semaphore_signal(barrier, inc=1, device_id=sibling, device_id_type=MESH)
    mine = pl.ds(pl.multiple_of(x * rows, rows), rows)
    loads = [
        pltpu.make_async_copy(points_hbm, layer_points.at[mine], load_sem.at[0]),
        pltpu.make_async_copy(probes_hbm, layer_probes.at[mine], load_sem.at[1]),
        pltpu.make_async_copy(points_hbm.at[own_rows], visitors.at[z], load_sem.at[2]),
    ]
    for load in loads:
        load.start()
    pl.semaphore_wait(barrier, jnp.where((z > 0) & (z < outer - 1), 2, 1) + inner - 1 + 1)

    for way in (1, -1):
        @pl.when(inside(z + way))
        def _(way=way):
            onward(z, way, 0, first=True).start()
            onward(z, way, 1, first=True).start()
    for part in range(2):
        for step in range(1, inner):
            for copy in across(step, part):
                copy.start()

    for load in loads:
        load.wait()
    prepare_rows(x, 0)
    prepare_rows(x, 1)
    prepare_visitor(z)
    pair(z, x, (0, 1), fresh=True)

    def both_ways(distance, work):
        def one(k, carry):
            layer = z + (1 - 2 * k) * distance

            @pl.when(inside(layer))
            def _():
                work(layer, 1 - 2 * k)
            return carry
        lax.fori_loop(0, 2, one, 0)

    def receive(distance, turn):
        def work(layer, way):
            wait_recv(visitors.at[layer, pl.ds(turn * (piece // 2), piece // 2)], visit_recv.at[layer, turn])

            @pl.when(inside(z - way))
            def _():
                onward(layer, -way, turn).start()
        both_ways(distance, work)

    def others(work):
        def one(step, carry):
            work(step, lax.rem(x + step, inner))
            return carry
        lax.fori_loop(1, inner, one, 0)

    def take_rows(part):
        def take(step, column):
            wait_rows(column, part, core)
            for copy in share(step, part):
                copy.start()
        others(take)

    def use_rows(part, reach):
        def use(step, column):
            wait_rows(column, part, 1 - core)
            prepare_rows(column, part)

            def one(k, carry):
                layer = z + k - reach

                @pl.when(inside(layer))
                def _():
                    pair(layer, column, (part,))
                    if part == 1:
                        @pl.when((layer != z) & (step == inner - 1))
                        def _():
                            back(layer, 0).start()
                            back(layer, 1).start()
                return carry
            lax.fori_loop(0, 2 * reach + 1, one, 0)
        others(use)

    def meet_own(layer, way):
        prepare_visitor(layer)
        pair(layer, x, (0, 1), fresh=True)

    near = min(2, outer - 1)
    receive(1, 0)
    receive(1, 1)
    both_ways(1, meet_own)
    take_rows(0)
    if near == 2:
        receive(2, 0)
    use_rows(0, 1)
    if near == 2:
        receive(2, 1)

        def meet_more(layer, way):
            meet_own(layer, way)
            others(lambda step, column: pair(layer, column, (0,)))
        both_ways(2, meet_more)
    take_rows(1)
    use_rows(1, near)

    def meet_all(layer, turn):
        here = dict(begin=turn * (piece // 2), count=piece // 2)
        prepare_visitor(layer, **here)
        for column in range(0, inner, 2):
            pair(layer, column, (0, 1, 2, 3), fresh=column == 0, **here)
        back(layer, turn).start()
    for distance in range(near + 1, outer):
        for turn in range(2):
            receive(distance, turn)
            both_ways(distance, lambda layer, way, turn=turn: meet_all(layer, turn))

    for way in (1, -1):
        @pl.when(inside(z + way))
        def _(way=way):
            onward(z, way, 0, first=True).wait_send()
            onward(z, way, 1, first=True).wait_send()

    def sent(layer, way):
        @pl.when(inside(z - way))
        def _():
            onward(layer, -way, 0).wait_send()
            onward(layer, -way, 1).wait_send()
    for distance in range(1, outer):
        both_ways(distance, sent)
    for part in range(2):
        for step in range(1, inner):
            for copy in across(step, part) + share(step, part):
                copy.wait_send()

    result = sums[z]
    for step in range(1, outer):
        layer = lax.rem(z + step, outer)
        for turn in range(2):
            wait_recv(returned.at[layer, pl.ds(turn * (piece // 2), piece // 2)], back_recv.at[layer, turn])
        result = result + returned[layer]
    out_ref[...] = result
    for step in range(1, outer):
        for turn in range(2):
            back(lax.rem(z + step, outer), turn).wait_send()


def body(points, probes):
    rows, width = points.shape
    count = probes.shape[1]
    blocks = lax.axis_size("blk")
    inner = 1 << ((blocks.bit_length() - 1) // 2)
    outer = blocks // inner
    piece = rows // lax.axis_size("team")
    f32, bf16 = jnp.float32, jnp.bfloat16
    dma = pltpu.SemaphoreType.DMA
    return pl.pallas_call(
        functools.partial(kernel, outer, inner),
        out_shape=jax.ShapeDtypeStruct((piece, count), f32),
        in_specs=[pl.BlockSpec(memory_space=pl.ANY)] * 2,
        out_specs=pl.BlockSpec(memory_space=pltpu.VMEM),
        scratch_shapes=[
            pltpu.VMEM((inner * rows, width), f32),
            pltpu.VMEM((inner * rows, count), f32),
            pltpu.VMEM((inner * rows, width), bf16),
            pltpu.VMEM((inner * rows, width), bf16),
            pltpu.VMEM((inner * rows, count), bf16),
            pltpu.VMEM((inner * rows, count), bf16),
            pltpu.VMEM((inner * 2, 1, rows // 2), f32),
            pltpu.VMEM((outer, piece, width), f32),
            pltpu.VMEM((outer, 2 * piece, width), bf16),
            pltpu.VMEM((outer, piece, 1), f32),
            pltpu.VMEM((outer, piece, count), f32),
            pltpu.VMEM((outer, piece, count), f32),
            dma((3,)),
            dma((outer, 2, 2)),
            dma((outer, 2)),
            dma((inner - 1, 2, 2)),
            dma((inner - 1, 2, 2)),
            dma((inner * 4, 2)),
            dma((outer, 2)),
            dma((outer, 2)),
        ],
        compiler_params=pltpu.CompilerParams(collective_id=0, has_side_effects=True),
    )(points, probes)


def solution(mesh):
    in_specs = (P("blk", None), P("blk", None))
    out_specs = P(("blk", "team"), None)
    return jax.shard_map(body, mesh=mesh, in_specs=in_specs, out_specs=out_specs, check_vma=False)
```

```python
import functools

import jax
import jax.numpy as jnp
from jax import lax
from jax.experimental import pallas as pl
from jax.experimental.pallas import tpu as pltpu
from jax.sharding import PartitionSpec as P

MESH = pl.DeviceIdType.MESH
CHUNKS = 4
CORES = 2


def kernel(
    outer,
    inner,
    teams,
    points_hbm,
    probes_hbm,
    out_ref,
    layer_all,
    visitors,
    visitor_vals,
    cols_high,
    cols_low,
    vals_high,
    vals_low,
    layer_sq,
    terms,
    visitor_sq,
    second,
    sums,
    returned,
    partial,
    scattered,
    load_sem,
    visit_send,
    visit_recv,
    direct_send,
    gift_send,
    gift_recv,
    row_send,
    plane_send,
    share_send,
    row_recv,
    back_send,
    back_recv,
    part_send,
    part_recv,
):
    sub, count = sums.shape[2:]
    width = layer_all.shape[-1] - count
    every = width + count
    half = outer // 2
    planes = teams // CORES
    wide = teams * sub
    step_rows = 2 * sub // CHUNKS
    scale = 2.0 / width
    block = lax.axis_index("blk")
    team = lax.axis_index("team")
    z = block // inner
    x = lax.rem(block, inner)
    plane = team // CORES
    core = lax.rem(team, CORES)
    left = z < half
    near = jnp.where(left, 1, -1)
    place = jnp.where(left, z, outer - 1 - z)

    def at(layer, column, member=None):
        target = {"blk": layer * inner + column}
        if member is not None:
            target["team"] = member
        return target

    def slot(layer):
        return jnp.where(layer < half, 2 * layer, 2 * (outer - 1 - layer) + 1)

    def inside(layer):
        return layer * (outer - 1 - layer) >= 0

    def remote(src, dst, send, recv, target):
        return pltpu.make_async_remote_copy(
            src_ref=src, dst_ref=dst, send_sem=send, recv_sem=recv, device_id=target, device_id_type=MESH
        )

    def wait_recv(ref, sem):
        pltpu.make_async_copy(ref, ref, sem).wait()

    def chunk(k):
        return (k * 2) // CHUNKS, pl.ds((k % (CHUNKS // 2)) * step_rows, step_rows)


    def same_side(layer, way):
        return (layer < half) if way == 1 else (layer >= half)

    def visit(layer, way, k, first, op):
        part, rows = chunk(k)
        dst = visitors.at[part, slot(layer), rows]

        op(remote(
            layer_all.at[part, x, team, rows, pl.ds(0, width)] if first else dst,
            dst,
            visit_send.at[layer, (way + 1) // 2, k],
            visit_recv.at[layer, k],
            at(z + way, x),
        ))

    def start(copy):
        copy.start()

    def wait_send(copy):
        copy.wait_send()

    last = CHUNKS - 1

    def is_end(layer):
        return (layer == 0) | (layer == outer - 1)

    def own_visits(way, k, op):
        first, final = (0, outer - 2) if way == 1 else (1, outer - 1)
        if k >= CHUNKS // 2:
            first, final = (0, half - 1) if way == 1 else (half, outer - 1)
        if k == last:
            first, final = (0, 0) if way == 1 else (outer - 1, outer - 1)

        @pl.when((z - first) * (final - z) >= 0)
        def _():
            visit(z, way, k, True, op)

    def goes_on(layer, way, k):
        low, high = (0, outer - 2) if way == 1 else (1, outer - 1)
        first, final = 0, outer - 1
        if k >= CHUNKS // 2:
            first, final = (0, half - 1) if way == 1 else (half, outer - 1)
        if k == last:
            first, final = (0, 0) if way == 1 else (outer - 1, outer - 1)
        return jnp.minimum((layer - first) * (final - layer), (z - low) * (high - z)) >= 0

    def wait_visit(layer, k):
        part, rows = chunk(k)
        wait_recv(visitors.at[part, slot(layer), rows], visit_recv.at[layer, k])

    def forward(distance, k):
        for way in (1, -1):
            layer = z - way * distance

            @pl.when(goes_on(layer, way, k))
            def _(way=way, layer=layer):
                wait_visit(layer, k)
                visit(layer, way, k, False, start)

    def settle(layer, part):
        onward = ((layer < z) & (z + 1 < outer)) | ((layer > z) & (z > 0))
        for k in range(part * CHUNKS // 2, (part + 1) * CHUNKS // 2):
            sent_on = onward & is_end(layer) if k == last else onward
            waiting = visits_me(layer, part) & jnp.logical_not(sent_on)

            @pl.when(waiting)
            def _(k=k):
                wait_visit(layer, k)

    def direct(op):
        part, rows = chunk(last)
        for distance in range(outer - 1, 0, -1):
            @pl.when(jnp.minimum(place - 1, (z + near * distance) * (outer - 1 - z - near * distance)) >= 0)
            def _(distance=distance):
                op(remote(
                    layer_all.at[part, x, team, rows, pl.ds(0, width)],
                    visitors.at[part, slot(z), rows],
                    direct_send.at[distance],
                    visit_recv.at[z, last],
                    at(z + near * distance, x),
                ))

    def gift(op):
        for distance in range(1, half):
            @pl.when(place + distance < half)
            def _(distance=distance):
                op(remote(
                    layer_all.at[:, x, team, :, pl.ds(width, count)],
                    visitor_vals.at[:, slot(z)],
                    gift_send.at[distance],
                    gift_recv.at[z],
                    at(z + near * distance, x),
                ))


    def piece(column, member, k):
        part, rows = chunk(k)
        return layer_all.at[part, column, member, rows]

    def arrives(k, other):
        return k == CHUNKS - 1 or other == 0

    def member_of(other):
        return lax.rem(plane + other, planes) * CORES + core

    def across(step, k):
        return [
            remote(
                piece(x, member_of(other), k),
                piece(x, member_of(other), k),
                row_send.at[step - 1, k + other],
                row_recv.at[x, member_of(other), k],
                at(z, lax.rem(x + step, inner)),
            )
            for other in range(planes)
            if arrives(k, other)
        ]

    def along(step, k, other):
        column = lax.rem(x + step, inner)
        return remote(
            piece(column, team, k),
            piece(column, team, k),
            plane_send.at[step - 1, other - 1, k],
            row_recv.at[column, team, k],
            at(z, x, member_of(other)),
        )

    def share(step, k, other):
        column = lax.rem(x + step, inner)
        return remote(
            piece(column, member_of(other), k),
            piece(column, member_of(other), k),
            share_send.at[step - 1, other, k],
            row_recv.at[column, member_of(other), k],
            at(z, x, team + 1 - 2 * core),
        )

    def others(work):
        if inner == 2:
            work(1, 1 - x)
            return

        def one(step, carry):
            work(step, lax.rem(x + step, inner))
            return carry
        lax.fori_loop(1, inner, one, 0)

    def wait_piece(column, member, k):
        wait_recv(piece(column, member, k), row_recv.at[column, member, k])

    def take_across(k):
        def take(step, column):
            for other in range(planes):
                if arrives(k, other):
                    wait_piece(column, member_of(other), k)
                    if k < CHUNKS - 1:
                        for further in range(1, planes):
                            along(step, k, further).start()
                    share(step, k, other).start()
        others(take)

    def take_along(k):
        def take(step, column):
            for other in range(1, planes):
                wait_piece(column, member_of(other), k)
                share(step, k, other).start()
        others(take)

    def take_shared(k):
        def take(step, column):
            for other in range(planes):
                wait_piece(column, member_of(other) + 1 - 2 * core, k)
        others(take)


    def back(layer, part):
        return remote(
            sums.at[part, slot(layer)],
            returned.at[part, slot(z)],
            back_send.at[part, layer],
            back_recv.at[part, z],
            at(layer, x),
        )

    def visits_me(layer, part):
        if part == 0:
            return layer != z
        return ((layer < half) & (layer < z)) | ((layer >= half) & (layer > z))

    def i_visit(layer, part):
        if part == 0:
            return layer != z
        return (left & (layer > z)) | (jnp.logical_not(left) & (layer < z))

    def scatter(step):
        index = lax.rem(x * teams + team + step, inner * teams)
        return remote(
            partial.at[index // teams, lax.rem(index, teams)],
            scattered.at[x * teams + team],
            part_send.at[index],
            part_recv.at[x * teams + team],
            at(z, index // teams, lax.rem(index, teams)),
        )


    def two_terms(values):
        high = values.astype(jnp.bfloat16)
        return high, (values - high.astype(jnp.float32)).astype(jnp.bfloat16)

    def four_products(stacked, high, low, contract):
        rows = stacked.shape[0] // 2
        dot = functools.partial(
            lax.dot_general,
            dimension_numbers=(contract, ((), ())),
            preferred_element_type=jnp.float32,
        )
        by_high, by_low = dot(stacked, high), dot(stacked, low)
        return by_high[:rows] + (by_high[rows:] + by_low[:rows] + by_low[rows:])

    def prepare_columns(part, column):
        where = slice(part * wide, (part + 1) * wide)
        values = layer_all[part, column, :, :, 0:width].reshape(wide, width)
        total = jnp.sum(values * values, axis=1, keepdims=True)
        layer_sq[column, :, where] = jnp.broadcast_to(total, (wide, 128)).T[0:1, :]
        cols_high[column, where], cols_low[column, where] = two_terms(values)
        rest = layer_all[part, column, :, :, width:every].reshape(wide, count)
        vals_high[column, where], vals_low[column, where] = two_terms(rest)

    def prepare_rows(part, layer, values):
        where = pl.ds(pl.multiple_of(slot(layer) * sub, sub), sub)
        visitor_sq[part, where] = jnp.sum(values * values, axis=1, keepdims=True)
        high, low = two_terms(values)
        terms[part, 0, where, :] = high
        terms[part, 1, where, :] = low

    def pair(part, begin, size, column, fresh):
        rows = pl.ds(begin * sub if isinstance(begin, int) else pl.multiple_of(begin * sub, 2 * sub), size * sub)
        cross = four_products(
            terms[part, :, rows, :].reshape(2 * size * sub, width),
            cols_high[column],
            cols_low[column],
            ((1,), (1,)),
        )
        arg = (visitor_sq[part, rows] + layer_sq[column] - 2.0 * cross) * scale
        value = jnp.exp(-jnp.maximum(arg, 0.0))
        second[part, rows, pl.ds(pl.multiple_of(column * wide, wide), wide)] = value[:, wide:]
        product = four_products(
            jnp.concatenate(two_terms(value), axis=0), vals_high[column], vals_low[column], ((1,), (0,))
        ).reshape(size, sub, count)
        kept = pl.ds(begin, size)
        sums[part, kept] = product if fresh else sums[part, kept] + product

    def outward(index):
        layer = jnp.where(left, index, outer - 1 - index)
        where = pl.ds(pl.multiple_of(slot(layer) * sub, sub), sub)
        wait_recv(visitor_vals.at[:, slot(layer)], gift_recv.at[layer])
        value = jnp.concatenate([second[0, where, :], second[1, where, :]], axis=0).T
        rest = jnp.concatenate([visitor_vals[part, slot(layer)] for part in range(2)], axis=0)
        high, low = two_terms(rest)
        product = four_products(jnp.concatenate(two_terms(value), axis=0), high, low, ((1,), (0,)))
        product = product.reshape(inner, teams, sub, count)
        partial[...] = product if index == 0 else partial[...] + product


    loads = [
        pltpu.make_async_copy(
            source.at[:, part], layer_all.at[part, x, :, :, pl.ds(begin, extent)], load_sem.at[part, which]
        )
        for part in range(2)
        for which, (source, begin, extent) in enumerate(((points_hbm, 0, width), (probes_hbm, width, count)))
    ]
    barrier = pltpu.get_barrier_semaphore()

    def greet(target):
        pl.semaphore_signal(barrier, inc=1, device_id=target, device_id_type=MESH)

    for way in (1, -1):
        @pl.when(inside(z + way))
        def _(way=way):
            greet(at(z + way, x))
    for step in range(1, inner):
        greet(at(z, lax.rem(x + step, inner)))
    for other in range(1, planes):
        greet(at(z, x, member_of(other)))
    greet(at(z, x, team + 1 - 2 * core))
    for load in loads:
        load.start()
    for load in loads:
        load.wait()
    pl.semaphore_wait(barrier, jnp.where(is_end(z), 1, 2) + inner - 1 + planes)

    for k in range(CHUNKS):
        for way in (1, -1):
            own_visits(way, k, start)
        for step in range(1, inner):
            for copy in across(step, k):
                copy.start()
    gift(start)

    for part in range(2):
        prepare_columns(part, x)
        prepare_rows(part, z, layer_all[part, x, team, :, 0:width])

    for k in range(last):
        forward(1, k)
        take_across(k)
    forward(1, last)
    direct(start)
    for k in range(2):
        if outer > 3:
            forward(2, k)
        take_along(k)
    if outer > 3:
        forward(2, 2)
    take_across(last)
    take_along(2)
    if outer > 3:
        forward(2, last)
    for distance in range(3, outer - 1):
        for k in range(CHUNKS):
            forward(distance, k)

    for step in range(1, outer):
        layer = lax.rem(z + step, outer)
        settle(layer, 0)
        prepare_rows(0, layer, visitors[0, slot(layer)])
    pair(0, 0, outer, x, True)
    for k in range(CHUNKS):
        take_shared(k)
        if k == 1:
            others(lambda step, column: prepare_columns(0, column))
    others(lambda step, column: prepare_columns(1, column))
    others(lambda step, column: pair(0, 0, outer, column, False))
    for step in range(1, outer):
        back(lax.rem(z + step, outer), 0).start()
    for order in range(half):
        index = jnp.where(place == 0, half - 1 - order, order)
        for layer in (index, outer - 1 - index):
            settle(layer, 1)

            @pl.when(visits_me(layer, 1))
            def _(layer=layer):
                prepare_rows(1, layer, visitors[1, slot(layer)])
        pair(1, 2 * index, 2, x, True)
        others(lambda step, column, index=index: pair(1, 2 * index, 2, column, False))
        for layer in (index, outer - 1 - index):
            @pl.when(visits_me(layer, 1))
            def _(layer=layer):
                back(layer, 1).start()
        if order < half - 1:
            @pl.when(place > order)
            def _(order=order):
                outward(order)

            @pl.when(place == order + 1)
            def _():
                for step in range(1, inner * teams):
                    scatter(step).start()


    for way in (1, -1):
        for k in range(CHUNKS):
            own_visits(way, k, wait_send)
            for distance in range(1, outer - 1):
                layer = z - way * distance

                @pl.when(goes_on(layer, way, k))
                def _(way=way, k=k, layer=layer):
                    visit(layer, way, k, False, wait_send)
    direct(wait_send)
    gift(wait_send)

    def sent(step, column):
        for k in range(CHUNKS):
            for copy in across(step, k):
                copy.wait_send()
            for other in range(planes):
                if other > 0 and k < CHUNKS - 1:
                    along(step, k, other).wait_send()
                share(step, k, other).wait_send()
    others(sent)


    mine = slot(z)
    for part in range(2):
        result = sums[part, mine]
        if part == 0:
            for step in range(1, outer):
                layer = lax.rem(z + step, outer)
                wait_recv(returned.at[0, slot(layer)], back_recv.at[0, layer])
                result = result + returned[0, slot(layer)]
            out_ref[0] = result
        else:
            out_ref[1] = result
            for step in range(1, outer):
                layer = lax.rem(z + step, outer)

                @pl.when(i_visit(layer, 1))
                def _(layer=layer):
                    wait_recv(returned.at[1, slot(layer)], back_recv.at[1, layer])
                    out_ref[1] = out_ref[1] + returned[1, slot(layer)]

            @pl.when(place > 0)
            def _():
                own = x * teams + team
                total = out_ref[1] + partial[x, team]
                for step in range(1, inner * teams):
                    index = lax.rem(own + step, inner * teams)
                    wait_recv(scattered.at[index], part_recv.at[index])
                    total = total + scattered[index]
                out_ref[1] = total
                for step in range(1, inner * teams):
                    scatter(step).wait_send()
    for step in range(1, outer):
        layer = lax.rem(z + step, outer)
        for part in range(2):
            @pl.when(visits_me(layer, part))
            def _(layer=layer, part=part):
                back(layer, part).wait_send()


def body(points, probes):
    rows, width = points.shape
    count = probes.shape[1]
    blocks, teams = lax.axis_size("blk"), lax.axis_size("team")
    inner = 1 << ((blocks.bit_length() - 1) // 2)
    outer = blocks // inner
    sub = rows // teams // 2
    every = width + count
    f32, bf16 = jnp.float32, jnp.bfloat16
    dma = pltpu.SemaphoreType.DMA
    planes = teams // CORES
    result = pl.pallas_call(
        functools.partial(kernel, outer, inner, teams),
        out_shape=jax.ShapeDtypeStruct((2, sub, count), f32),
        in_specs=[pl.BlockSpec(memory_space=pl.ANY)] * 2,
        out_specs=pl.BlockSpec(memory_space=pltpu.VMEM),
        scratch_shapes=[
            pltpu.VMEM((2, inner, teams, sub, every), f32),
            pltpu.VMEM((2, outer, sub, width), f32),
            pltpu.VMEM((2, outer, sub, count), f32),
            pltpu.VMEM((inner, 2 * teams * sub, width), bf16),
            pltpu.VMEM((inner, 2 * teams * sub, width), bf16),
            pltpu.VMEM((inner, 2 * teams * sub, count), bf16),
            pltpu.VMEM((inner, 2 * teams * sub, count), bf16),
            pltpu.VMEM((inner, 1, 2 * teams * sub), f32),
            pltpu.VMEM((2, 2, outer * sub, width), bf16),
            pltpu.VMEM((2, outer * sub, 1), f32),
            pltpu.VMEM((2, outer * sub, inner * teams * sub), f32),
            pltpu.VMEM((2, outer, sub, count), f32),
            pltpu.VMEM((2, outer, sub, count), f32),
            pltpu.VMEM((inner, teams, sub, count), f32),
            pltpu.VMEM((inner * teams, sub, count), f32),
            dma((2, 2)),
            dma((outer, 2, CHUNKS)),
            dma((outer, CHUNKS)),
            dma((outer,)),
            dma((outer,)),
            dma((outer,)),
            dma((inner - 1, CHUNKS + planes - 1)),
            dma((inner - 1, planes - 1, CHUNKS)),
            dma((inner - 1, planes, CHUNKS)),
            dma((inner, teams, CHUNKS)),
            dma((2, outer)),
            dma((2, outer)),
            dma((inner * teams,)),
            dma((inner * teams,)),
        ],
        compiler_params=pltpu.CompilerParams(
            collective_id=0, has_side_effects=True, vmem_limit_bytes=60 * 2**20
        ),
    )(points.reshape(teams, 2, sub, width), probes.reshape(teams, 2, sub, count))
    return result.reshape(2 * sub, count)


def solution(mesh):
    in_specs = (P("blk", None), P("blk", None))
    out_specs = P(("blk", "team"), None)
    return jax.shard_map(body, mesh=mesh, in_specs=in_specs, out_specs=out_specs, check_vma=False)
```

```python
import functools

import jax
import jax.numpy as jnp
from jax import lax
from jax.experimental import pallas as pl
from jax.experimental.pallas import tpu as pltpu
from jax.sharding import PartitionSpec as P

MESH = pl.DeviceIdType.MESH
CHUNKS = 4
CORES = 2


def kernel(
    outer,
    inner,
    teams,
    points_hbm,
    probes_hbm,
    out_ref,
    layer_all,
    visitors,
    visitor_vals,
    cols_high,
    cols_low,
    vals_high,
    vals_low,
    layer_sq,
    terms,
    visitor_sq,
    second,
    sums,
    returned,
    partial,
    scattered,
    load_sem,
    visit_send,
    visit_recv,
    direct_send,
    gift_send,
    gift_recv,
    row_send,
    plane_send,
    share_send,
    row_recv,
    back_send,
    back_recv,
    part_send,
    part_recv,
):
    sub, count = sums.shape[2:]
    width = layer_all.shape[-1] - count
    every = width + count
    half = outer // 2
    planes = teams // CORES
    wide = teams * sub
    step_rows = 2 * sub // CHUNKS
    scale = 2.0 / width
    block = lax.axis_index("blk")
    team = lax.axis_index("team")
    z = block // inner
    x = lax.rem(block, inner)
    plane = team // CORES
    core = lax.rem(team, CORES)
    left = z < half
    near = jnp.where(left, 1, -1)
    place = jnp.where(left, z, outer - 1 - z)

    def at(layer, column, member=None):
        target = {"blk": layer * inner + column}
        if member is not None:
            target["team"] = member
        return target

    def slot(layer):
        return jnp.where(layer < half, 2 * layer, 2 * (outer - 1 - layer) + 1)

    def inside(layer):
        return layer * (outer - 1 - layer) >= 0

    def remote(src, dst, send, recv, target):
        return pltpu.make_async_remote_copy(
            src_ref=src, dst_ref=dst, send_sem=send, recv_sem=recv, device_id=target, device_id_type=MESH
        )

    def wait_recv(ref, sem):
        pltpu.make_async_copy(ref, ref, sem).wait()

    def chunk(k):
        return (k * 2) // CHUNKS, pl.ds((k % (CHUNKS // 2)) * step_rows, step_rows)


    def same_side(layer, way):
        return (layer < half) if way == 1 else (layer >= half)

    def visit(layer, way, k, first, op):
        part, rows = chunk(k)
        dst = visitors.at[part, slot(layer), rows]

        op(remote(
            layer_all.at[part, x, team, rows, pl.ds(0, width)] if first else dst,
            dst,
            visit_send.at[layer, (way + 1) // 2, k],
            visit_recv.at[layer, k],
            at(z + way, x),
        ))

    def start(copy):
        copy.start()

    def wait_send(copy):
        copy.wait_send()

    last = CHUNKS - 1

    def is_end(layer):
        return (layer == 0) | (layer == outer - 1)

    def own_visits(way, k, op):
        first, final = (0, outer - 2) if way == 1 else (1, outer - 1)
        if k >= CHUNKS // 2:
            first, final = (0, half - 1) if way == 1 else (half, outer - 1)
        if k == last:
            first, final = (0, 0) if way == 1 else (outer - 1, outer - 1)

        @pl.when((z - first) * (final - z) >= 0)
        def _():
            visit(z, way, k, True, op)

    def goes_on(layer, way, k):
        low, high = (0, outer - 2) if way == 1 else (1, outer - 1)
        first, final = 0, outer - 1
        if k >= CHUNKS // 2:
            first, final = (0, half - 1) if way == 1 else (half, outer - 1)
        if k == last:
            first, final = (0, 0) if way == 1 else (outer - 1, outer - 1)
        return jnp.minimum((layer - first) * (final - layer), (z - low) * (high - z)) >= 0

    def wait_visit(layer, k):
        part, rows = chunk(k)
        wait_recv(visitors.at[part, slot(layer), rows], visit_recv.at[layer, k])

    def forward(distance, k):
        for way in (1, -1):
            layer = z - way * distance

            @pl.when(goes_on(layer, way, k))
            def _(way=way, layer=layer):
                wait_visit(layer, k)
                visit(layer, way, k, False, start)

    def settle(layer, part):
        onward = ((layer < z) & (z + 1 < outer)) | ((layer > z) & (z > 0))
        for k in range(part * CHUNKS // 2, (part + 1) * CHUNKS // 2):
            sent_on = onward & is_end(layer) if k == last else onward
            waiting = visits_me(layer, part) & jnp.logical_not(sent_on)

            @pl.when(waiting)
            def _(k=k):
                wait_visit(layer, k)

    def direct(op):
        part, rows = chunk(last)
        for distance in range(outer - 1, 0, -1):
            @pl.when(jnp.minimum(place - 1, (z + near * distance) * (outer - 1 - z - near * distance)) >= 0)
            def _(distance=distance):
                op(remote(
                    layer_all.at[part, x, team, rows, pl.ds(0, width)],
                    visitors.at[part, slot(z), rows],
                    direct_send.at[distance],
                    visit_recv.at[z, last],
                    at(z + near * distance, x),
                ))

    def gift(op):
        for distance in range(1, half):
            @pl.when(place + distance < half)
            def _(distance=distance):
                op(remote(
                    layer_all.at[:, x, team, :, pl.ds(width, count)],
                    visitor_vals.at[:, slot(z)],
                    gift_send.at[distance],
                    gift_recv.at[z],
                    at(z + near * distance, x),
                ))


    def piece(column, member, k):
        part, rows = chunk(k)
        return layer_all.at[part, column, member, rows]

    def arrives(k, other):
        return k == CHUNKS - 1 or other == 0

    def member_of(other):
        return lax.rem(plane + other, planes) * CORES + core

    def across(step, k):
        return [
            remote(
                piece(x, member_of(other), k),
                piece(x, member_of(other), k),
                row_send.at[step - 1, k + other],
                row_recv.at[x, member_of(other), k],
                at(z, lax.rem(x + step, inner)),
            )
            for other in range(planes)
            if arrives(k, other)
        ]

    def along(step, k, other):
        column = lax.rem(x + step, inner)
        return remote(
            piece(column, team, k),
            piece(column, team, k),
            plane_send.at[step - 1, other - 1, k],
            row_recv.at[column, team, k],
            at(z, x, member_of(other)),
        )

    def share(step, k, other):
        column = lax.rem(x + step, inner)
        return remote(
            piece(column, member_of(other), k),
            piece(column, member_of(other), k),
            share_send.at[step - 1, other, k],
            row_recv.at[column, member_of(other), k],
            at(z, x, team + 1 - 2 * core),
        )

    def others(work):
        if inner == 2:
            work(1, 1 - x)
            return

        def one(step, carry):
            work(step, lax.rem(x + step, inner))
            return carry
        lax.fori_loop(1, inner, one, 0)

    def wait_piece(column, member, k):
        wait_recv(piece(column, member, k), row_recv.at[column, member, k])

    def take_across(k):
        def take(step, column):
            for other in range(planes):
                if arrives(k, other):
                    wait_piece(column, member_of(other), k)
                    if k < CHUNKS - 1:
                        for further in range(1, planes):
                            along(step, k, further).start()
                    share(step, k, other).start()
        others(take)

    def take_along(k):
        def take(step, column):
            for other in range(1, planes):
                wait_piece(column, member_of(other), k)
                share(step, k, other).start()
        others(take)

    def take_shared(k):
        def take(step, column):
            for other in range(planes):
                wait_piece(column, member_of(other) + 1 - 2 * core, k)
        others(take)


    def back(layer, part):
        return remote(
            sums.at[part, slot(layer)],
            returned.at[part, slot(z)],
            back_send.at[part, layer],
            back_recv.at[part, z],
            at(layer, x),
        )

    def visits_me(layer, part):
        if part == 0:
            return layer != z
        return ((layer < half) & (layer < z)) | ((layer >= half) & (layer > z))

    def i_visit(layer, part):
        if part == 0:
            return layer != z
        return (left & (layer > z)) | (jnp.logical_not(left) & (layer < z))

    def scatter(step):
        index = lax.rem(x * teams + team + step, inner * teams)
        return remote(
            partial.at[index // teams, lax.rem(index, teams)],
            scattered.at[x * teams + team],
            part_send.at[index],
            part_recv.at[x * teams + team],
            at(z, index // teams, lax.rem(index, teams)),
        )


    def two_terms(values):
        high = values.astype(jnp.bfloat16)
        return high, (values - high.astype(jnp.float32)).astype(jnp.bfloat16)

    def four_products(stacked, high, low, contract):
        rows = stacked.shape[0] // 2
        dot = functools.partial(
            lax.dot_general,
            dimension_numbers=(contract, ((), ())),
            preferred_element_type=jnp.float32,
        )
        by_high, by_low = dot(stacked, high), dot(stacked, low)
        return by_high[:rows] + (by_high[rows:] + by_low[:rows] + by_low[rows:])

    def prepare_columns(part, column):
        where = slice(part * wide, (part + 1) * wide)
        values = layer_all[part, column, :, :, 0:width].reshape(wide, width)
        total = jnp.sum(values * values, axis=1, keepdims=True)
        layer_sq[column, :, where] = jnp.broadcast_to(total, (wide, 128)).T[0:1, :]
        cols_high[column, where], cols_low[column, where] = two_terms(values)
        rest = layer_all[part, column, :, :, width:every].reshape(wide, count)
        vals_high[column, where], vals_low[column, where] = two_terms(rest)

    def prepare_rows(part, layer, values):
        where = pl.ds(pl.multiple_of(slot(layer) * sub, sub), sub)
        visitor_sq[part, where] = jnp.sum(values * values, axis=1, keepdims=True)
        high, low = two_terms(values)
        terms[part, 0, where, :] = high
        terms[part, 1, where, :] = low

    def pair(part, begin, size, column, fresh):
        rows = pl.ds(begin * sub if isinstance(begin, int) else pl.multiple_of(begin * sub, 2 * sub), size * sub)
        cross = four_products(
            terms[part, :, rows, :].reshape(2 * size * sub, width),
            cols_high[column],
            cols_low[column],
            ((1,), (1,)),
        )
        arg = (visitor_sq[part, rows] + layer_sq[column] - 2.0 * cross) * scale
        value = jnp.exp(-jnp.maximum(arg, 0.0))
        second[part, rows, pl.ds(pl.multiple_of(column * wide, wide), wide)] = value[:, wide:]
        product = four_products(
            jnp.concatenate(two_terms(value), axis=0), vals_high[column], vals_low[column], ((1,), (0,))
        ).reshape(size, sub, count)
        kept = pl.ds(begin, size)
        sums[part, kept] = product if fresh else sums[part, kept] + product

    def outward(index):
        layer = jnp.where(left, index, outer - 1 - index)
        where = pl.ds(pl.multiple_of(slot(layer) * sub, sub), sub)
        wait_recv(visitor_vals.at[:, slot(layer)], gift_recv.at[layer])
        value = jnp.concatenate([second[0, where, :], second[1, where, :]], axis=0).T
        rest = jnp.concatenate([visitor_vals[part, slot(layer)] for part in range(2)], axis=0)
        high, low = two_terms(rest)
        product = four_products(jnp.concatenate(two_terms(value), axis=0), high, low, ((1,), (0,)))
        product = product.reshape(inner, teams, sub, count)
        partial[...] = product if index == 0 else partial[...] + product


    loads = [
        pltpu.make_async_copy(
            source.at[:, part], layer_all.at[part, x, :, :, pl.ds(begin, extent)], load_sem.at[part, which]
        )
        for part in range(2)
        for which, (source, begin, extent) in enumerate(((points_hbm, 0, width), (probes_hbm, width, count)))
    ]
    barrier = pltpu.get_barrier_semaphore()

    def greet(target):
        pl.semaphore_signal(barrier, inc=1, device_id=target, device_id_type=MESH)

    for way in (1, -1):
        @pl.when(inside(z + way))
        def _(way=way):
            greet(at(z + way, x))
    for step in range(1, inner):
        greet(at(z, lax.rem(x + step, inner)))
    for other in range(1, planes):
        greet(at(z, x, member_of(other)))
    greet(at(z, x, team + 1 - 2 * core))
    for load in loads:
        load.start()
    for load in loads:
        load.wait()
    pl.semaphore_wait(barrier, jnp.where(is_end(z), 1, 2) + inner - 1 + planes)

    for k in range(CHUNKS):
        for way in (1, -1):
            own_visits(way, k, start)
        for step in range(1, inner):
            for copy in across(step, k):
                copy.start()
    gift(start)

    for part in range(2):
        prepare_columns(part, x)
        prepare_rows(part, z, layer_all[part, x, team, :, 0:width])

    for k in range(last):
        forward(1, k)
        take_across(k)
    forward(1, last)
    direct(start)
    for k in range(2):
        if outer > 3:
            forward(2, k)
        take_along(k)
    if outer > 3:
        forward(2, 2)
    take_across(last)
    take_along(2)
    if outer > 3:
        forward(2, last)
    for distance in range(3, outer - 1):
        for k in range(CHUNKS):
            forward(distance, k)

    for step in range(1, outer):
        layer = lax.rem(z + step, outer)
        settle(layer, 0)
        prepare_rows(0, layer, visitors[0, slot(layer)])
    pair(0, 0, outer, x, True)
    for k in range(CHUNKS):
        take_shared(k)
        if k == 1:
            others(lambda step, column: prepare_columns(0, column))
    others(lambda step, column: prepare_columns(1, column))
    others(lambda step, column: pair(0, 0, outer, column, False))
    for step in range(1, outer):
        back(lax.rem(z + step, outer), 0).start()
    for order in range(half):
        index = jnp.where(place == 0, half - 1 - order, order)
        for layer in (index, outer - 1 - index):
            settle(layer, 1)

            @pl.when(visits_me(layer, 1))
            def _(layer=layer):
                prepare_rows(1, layer, visitors[1, slot(layer)])
        pair(1, 2 * index, 2, x, True)
        others(lambda step, column, index=index: pair(1, 2 * index, 2, column, False))
        for layer in (index, outer - 1 - index):
            @pl.when(visits_me(layer, 1))
            def _(layer=layer):
                back(layer, 1).start()
        if order < half - 1:
            @pl.when(place > order)
            def _(order=order):
                outward(order)

            @pl.when(place == order + 1)
            def _():
                for step in range(1, inner * teams):
                    scatter(step).start()


    for way in (1, -1):
        for k in range(CHUNKS):
            own_visits(way, k, wait_send)
            for distance in range(1, outer - 1):
                layer = z - way * distance

                @pl.when(goes_on(layer, way, k))
                def _(way=way, k=k, layer=layer):
                    visit(layer, way, k, False, wait_send)
    direct(wait_send)
    gift(wait_send)

    def sent(step, column):
        for k in range(CHUNKS):
            for copy in across(step, k):
                copy.wait_send()
            for other in range(planes):
                if other > 0 and k < CHUNKS - 1:
                    along(step, k, other).wait_send()
                share(step, k, other).wait_send()
    others(sent)


    mine = slot(z)
    for part in range(2):
        result = sums[part, mine]
        if part == 0:
            for step in range(1, outer):
                layer = lax.rem(z + step, outer)
                wait_recv(returned.at[0, slot(layer)], back_recv.at[0, layer])
                result = result + returned[0, slot(layer)]
            out_ref[0] = result
        else:
            out_ref[1] = result
            for step in range(1, outer):
                layer = lax.rem(z + step, outer)

                @pl.when(i_visit(layer, 1))
                def _(layer=layer):
                    wait_recv(returned.at[1, slot(layer)], back_recv.at[1, layer])
                    out_ref[1] = out_ref[1] + returned[1, slot(layer)]

            @pl.when(place > 0)
            def _():
                own = x * teams + team
                total = out_ref[1] + partial[x, team]
                for step in range(1, inner * teams):
                    index = lax.rem(own + step, inner * teams)
                    wait_recv(scattered.at[index], part_recv.at[index])
                    total = total + scattered[index]
                out_ref[1] = total
                for step in range(1, inner * teams):
                    scatter(step).wait_send()
    for step in range(1, outer):
        layer = lax.rem(z + step, outer)
        for part in range(2):
            @pl.when(visits_me(layer, part))
            def _(layer=layer, part=part):
                back(layer, part).wait_send()


def body(points, probes):
    rows, width = points.shape
    count = probes.shape[1]
    blocks, teams = lax.axis_size("blk"), lax.axis_size("team")
    inner = 1 << ((blocks.bit_length() - 1) // 2)
    outer = blocks // inner
    sub = rows // teams // 2
    every = width + count
    f32, bf16 = jnp.float32, jnp.bfloat16
    dma = pltpu.SemaphoreType.DMA
    planes = teams // CORES
    result = pl.pallas_call(
        functools.partial(kernel, outer, inner, teams),
        out_shape=jax.ShapeDtypeStruct((2, sub, count), f32),
        in_specs=[pl.BlockSpec(memory_space=pl.ANY)] * 2,
        out_specs=pl.BlockSpec(memory_space=pltpu.VMEM),
        scratch_shapes=[
            pltpu.VMEM((2, inner, teams, sub, every), f32),
            pltpu.VMEM((2, outer, sub, width), f32),
            pltpu.VMEM((2, outer, sub, count), f32),
            pltpu.VMEM((inner, 2 * teams * sub, width), bf16),
            pltpu.VMEM((inner, 2 * teams * sub, width), bf16),
            pltpu.VMEM((inner, 2 * teams * sub, count), bf16),
            pltpu.VMEM((inner, 2 * teams * sub, count), bf16),
            pltpu.VMEM((inner, 1, 2 * teams * sub), f32),
            pltpu.VMEM((2, 2, outer * sub, width), bf16),
            pltpu.VMEM((2, outer * sub, 1), f32),
            pltpu.VMEM((2, outer * sub, inner * teams * sub), f32),
            pltpu.VMEM((2, outer, sub, count), f32),
            pltpu.VMEM((2, outer, sub, count), f32),
            pltpu.VMEM((inner, teams, sub, count), f32),
            pltpu.VMEM((inner * teams, sub, count), f32),
            dma((2, 2)),
            dma((outer, 2, CHUNKS)),
            dma((outer, CHUNKS)),
            dma((outer,)),
            dma((outer,)),
            dma((outer,)),
            dma((inner - 1, CHUNKS + planes - 1)),
            dma((inner - 1, planes - 1, CHUNKS)),
            dma((inner - 1, planes, CHUNKS)),
            dma((inner, teams, CHUNKS)),
            dma((2, outer)),
            dma((2, outer)),
            dma((inner * teams,)),
            dma((inner * teams,)),
        ],
        compiler_params=pltpu.CompilerParams(
            collective_id=0, has_side_effects=True, vmem_limit_bytes=55100 * 2**10
        ),
    )(points.reshape(teams, 2, sub, width), probes.reshape(teams, 2, sub, count))
    return result.reshape(2 * sub, count)


def solution(mesh):
    in_specs = (P("blk", None), P("blk", None))
    out_specs = P(("blk", "team"), None)
    return jax.shard_map(body, mesh=mesh, in_specs=in_specs, out_specs=out_specs, check_vma=False)
```

```python
import functools

import jax
import jax.numpy as jnp
from jax import lax
from jax.experimental import pallas as pl
from jax.experimental.pallas import tpu as pltpu
from jax.sharding import PartitionSpec as P

MESH = pl.DeviceIdType.MESH
CHUNKS = 4
CORES = 2


def kernel(
    outer,
    inner,
    teams,
    points_hbm,
    probes_hbm,
    out_ref,
    layer_all,
    visitors,
    visitor_vals,
    cols_high,
    cols_low,
    vals_high,
    vals_low,
    layer_sq,
    terms,
    visitor_sq,
    second,
    sums,
    returned,
    partial,
    scattered,
    load_sem,
    visit_send,
    visit_recv,
    gift_send,
    gift_recv,
    row_send,
    plane_send,
    share_send,
    row_recv,
    back_send,
    back_recv,
    part_send,
    part_recv,
):
    sub, count = sums.shape[2:]
    width = layer_all.shape[-1] - count
    every = width + count
    half = outer // 2
    planes = teams // CORES
    wide = teams * sub
    step_rows = 2 * sub // CHUNKS
    scale = 2.0 / width
    block = lax.axis_index("blk")
    team = lax.axis_index("team")
    z = block // inner
    x = lax.rem(block, inner)
    plane = team // CORES
    core = lax.rem(team, CORES)
    left = z < half
    near = jnp.where(left, 1, -1)
    place = jnp.where(left, z, outer - 1 - z)

    def at(layer, column, member=None):
        target = {"blk": layer * inner + column}
        if member is not None:
            target["team"] = member
        return target

    def slot(layer):
        return jnp.where(layer < half, 2 * layer, 2 * (outer - 1 - layer) + 1)

    def inside(layer):
        return layer * (outer - 1 - layer) >= 0

    def remote(src, dst, send, recv, target):
        return pltpu.make_async_remote_copy(
            src_ref=src, dst_ref=dst, send_sem=send, recv_sem=recv, device_id=target, device_id_type=MESH
        )

    def wait_recv(ref, sem):
        pltpu.make_async_copy(ref, ref, sem).wait()

    def chunk(k):
        return (k * 2) // CHUNKS, pl.ds((k % (CHUNKS // 2)) * step_rows, step_rows)


    def same_side(layer, way):
        return (layer < half) if way == 1 else (layer >= half)

    def visit(layer, way, k, first, op):
        part, rows = chunk(k)
        dst = visitors.at[part, slot(layer), rows]

        op(remote(
            layer_all.at[part, x, team, rows, pl.ds(0, width)] if first else dst,
            dst,
            visit_send.at[layer, (way + 1) // 2, k],
            visit_recv.at[layer, k],
            at(z + way, x),
        ))

    def start(copy):
        copy.start()

    def wait_send(copy):
        copy.wait_send()

    last = CHUNKS - 1

    def rank(layer):
        return jnp.minimum(layer, outer - 1 - layer)

    def is_end(layer):
        return rank(layer) == 0

    def own_visits(way, k, op):
        first, final = (0, outer - 2) if way == 1 else (1, outer - 1)
        if k >= CHUNKS // 2:
            first, final = (0, half - 1) if way == 1 else (half, outer - 1)

        @pl.when((z - first) * (final - z) >= 0)
        def _():
            visit(z, way, k, True, op)

    def goes_on(layer, way, k):
        low, high = (0, outer - 2) if way == 1 else (1, outer - 1)
        first, final = 0, outer - 1
        if k < CHUNKS // 2:
            return jnp.minimum((layer - first) * (final - layer), (z - low) * (high - z)) >= 0
        first, final = (0, half - 1) if way == 1 else (half, outer - 1)
        room = outer - 1 - layer - (z + way) if way == 1 else layer + (z + way) - (outer - 1)
        return jnp.minimum((layer - first) * (final - layer), room) >= 0

    def wait_visit(layer, k):
        part, rows = chunk(k)
        wait_recv(visitors.at[part, slot(layer), rows], visit_recv.at[layer, k])

    def forward(distance, k):
        for way in (1, -1):
            layer = z - way * distance

            @pl.when(goes_on(layer, way, k))
            def _(way=way, layer=layer):
                wait_visit(layer, k)
                visit(layer, way, k, False, start)

    def asked(distance):
        return (place == 0) & (distance > 1) & (distance < outer - 1)

    def settle(layer, part):
        for k in range(part * CHUNKS // 2, (part + 1) * CHUNKS // 2):
            for way in (1, -1):
                ahead = way * (z - layer) > 0
                stays = ahead & jnp.logical_not(goes_on(layer, way, k))
                if part == 1:
                    stays = stays & (rank(layer) <= place)
                if k == 0:
                    stays = stays & jnp.logical_not(asked(way * (z - layer)))

                @pl.when(stays)
                def _(k=k):
                    wait_visit(layer, k)

    def gift(distance, op):
        @pl.when(distance <= outer - 2 - 2 * place)
        def _():
            op(remote(
                layer_all.at[:, x, team, :, pl.ds(width, count)],
                visitor_vals.at[:, slot(z)],
                gift_send.at[distance],
                gift_recv.at[z],
                at(z + near * distance, x),
            ))

    def gift_afar(distance):
        if distance < outer - 1:
            @pl.when(place == 0)
            def _():
                wait_visit(z + near * distance, 0)
            gift(distance, start)


    def piece(column, member, k):
        part, rows = chunk(k)
        return layer_all.at[part, column, member, rows]

    def arrives(k, other):
        return k == CHUNKS - 1 or other == 0

    def member_of(other):
        return lax.rem(plane + other, planes) * CORES + core

    def across(step, k):
        return [
            remote(
                piece(x, member_of(other), k),
                piece(x, member_of(other), k),
                row_send.at[step - 1, k + other],
                row_recv.at[x, member_of(other), k],
                at(z, lax.rem(x + step, inner)),
            )
            for other in range(planes)
            if arrives(k, other)
        ]

    def along(step, k, other):
        column = lax.rem(x + step, inner)
        return remote(
            piece(column, team, k),
            piece(column, team, k),
            plane_send.at[step - 1, other - 1, k],
            row_recv.at[column, team, k],
            at(z, x, member_of(other)),
        )

    def share(step, k, other):
        column = lax.rem(x + step, inner)
        return remote(
            piece(column, member_of(other), k),
            piece(column, member_of(other), k),
            share_send.at[step - 1, other, k],
            row_recv.at[column, member_of(other), k],
            at(z, x, team + 1 - 2 * core),
        )

    def others(work):
        if inner == 2:
            work(1, 1 - x)
            return

        def one(step, carry):
            work(step, lax.rem(x + step, inner))
            return carry
        lax.fori_loop(1, inner, one, 0)

    def wait_piece(column, member, k):
        wait_recv(piece(column, member, k), row_recv.at[column, member, k])

    def take_across(k):
        def take(step, column):
            for other in range(planes):
                if arrives(k, other):
                    wait_piece(column, member_of(other), k)
                    if k < CHUNKS - 1:
                        for further in range(1, planes):
                            along(step, k, further).start()
                    share(step, k, other).start()
        others(take)

    def take_along(k):
        def take(step, column):
            for other in range(1, planes):
                wait_piece(column, member_of(other), k)
                share(step, k, other).start()
        others(take)

    def take_shared(k):
        def take(step, column):
            for other in range(planes):
                wait_piece(column, member_of(other) + 1 - 2 * core, k)
        others(take)


    def back(layer, part):
        return remote(
            sums.at[part, slot(layer)],
            returned.at[part, slot(z)],
            back_send.at[part, layer],
            back_recv.at[part, z],
            at(layer, x),
        )

    def visits_me(layer, part):
        if part == 0:
            return layer != z
        return (layer != z) & (rank(layer) <= place)

    def i_visit(layer, part):
        if part == 0:
            return layer != z
        return (layer != z) & (place <= rank(layer))

    def scatter(step):
        index = lax.rem(x * teams + team + step, inner * teams)
        return remote(
            partial.at[index // teams, lax.rem(index, teams)],
            scattered.at[x * teams + team],
            part_send.at[index],
            part_recv.at[x * teams + team],
            at(z, index // teams, lax.rem(index, teams)),
        )


    def two_terms(values):
        high = values.astype(jnp.bfloat16)
        return high, (values - high.astype(jnp.float32)).astype(jnp.bfloat16)

    def four_products(stacked, high, low, contract):
        rows = stacked.shape[0] // 2
        dot = functools.partial(
            lax.dot_general,
            dimension_numbers=(contract, ((), ())),
            preferred_element_type=jnp.float32,
        )
        by_high, by_low = dot(stacked, high), dot(stacked, low)
        return by_high[:rows] + (by_high[rows:] + by_low[:rows] + by_low[rows:])

    def prepare_columns(part, column):
        where = slice(part * wide, (part + 1) * wide)
        values = layer_all[part, column, :, :, 0:width].reshape(wide, width)
        total = jnp.sum(values * values, axis=1, keepdims=True)
        layer_sq[column, :, where] = jnp.broadcast_to(total, (wide, 128)).T[0:1, :]
        cols_high[column, where], cols_low[column, where] = two_terms(values)
        rest = layer_all[part, column, :, :, width:every].reshape(wide, count)
        vals_high[column, where], vals_low[column, where] = two_terms(rest)

    def prepare_rows(part, layer, values):
        where = pl.ds(pl.multiple_of(slot(layer) * sub, sub), sub)
        visitor_sq[part, where] = jnp.sum(values * values, axis=1, keepdims=True)
        high, low = two_terms(values)
        terms[part, 0, where, :] = high
        terms[part, 1, where, :] = low

    def pair(part, begin, size, column, fresh):
        rows = slice(begin * sub, (begin + size) * sub)
        cross = four_products(
            terms[part, :, rows, :].reshape(2 * size * sub, width),
            cols_high[column],
            cols_low[column],
            ((1,), (1,)),
        )
        arg = (visitor_sq[part, rows] + layer_sq[column] - 2.0 * cross) * scale
        value = jnp.exp(-jnp.maximum(arg, 0.0))
        second[part, rows, pl.ds(pl.multiple_of(column * wide, wide), wide)] = value[:, wide:]
        product = four_products(
            jnp.concatenate(two_terms(value), axis=0), vals_high[column], vals_low[column], ((1,), (0,))
        ).reshape(size, sub, count)
        kept = slice(begin, begin + size)
        sums[part, kept] = product if fresh else sums[part, kept] + product

    def outward(index):
        for layer in (index, outer - 1 - index):
            wait_recv(visitor_vals.at[:, slot(layer)], gift_recv.at[layer])
        rows = slice(2 * index * sub, 2 * (index + 1) * sub)
        value = jnp.concatenate([second[0, rows, :], second[1, rows, :]], axis=0).T
        rest = visitor_vals[:, 2 * index : 2 * (index + 1)].reshape(4 * sub, count)
        high, low = two_terms(rest)
        product = four_products(jnp.concatenate(two_terms(value), axis=0), high, low, ((1,), (0,)))
        product = product.reshape(inner, teams, sub, count)
        partial[...] = product if index == 0 else partial[...] + product


    loads = [
        pltpu.make_async_copy(
            source.at[:, part], layer_all.at[part, x, :, :, pl.ds(begin, extent)], load_sem.at[part, which]
        )
        for part in range(2)
        for which, (source, begin, extent) in enumerate(((points_hbm, 0, width), (probes_hbm, width, count)))
    ]
    barrier = pltpu.get_barrier_semaphore()

    def greet(target):
        pl.semaphore_signal(barrier, inc=1, device_id=target, device_id_type=MESH)

    for way in (1, -1):
        @pl.when(inside(z + way))
        def _(way=way):
            greet(at(z + way, x))
    for step in range(1, inner):
        greet(at(z, lax.rem(x + step, inner)))
    for other in range(1, planes):
        greet(at(z, x, member_of(other)))
    greet(at(z, x, team + 1 - 2 * core))
    for load in loads:
        load.start()
    for load in loads:
        load.wait()
    pl.semaphore_wait(barrier, jnp.where(is_end(z), 1, 2) + inner - 1 + planes)

    for k in range(CHUNKS):
        for way in (1, -1):
            if k < CHUNKS // 2:
                own_visits(way, k, start)
            else:
                @pl.when(place == 0)
                def _(way=way, k=k):
                    own_visits(way, k, start)
        for step in range(1, inner):
            for copy in across(step, k):
                copy.start()
    gift(1, start)

    for part in range(2):
        prepare_columns(part, x)
        prepare_rows(part, z, layer_all[part, x, team, :, 0:width])

    def forward_far(k):
        if outer > 3:
            forward(2, k)

    for k in range(last):
        forward(1, k)
        take_across(k)
    forward(1, last)

    @pl.when(place > 0)
    def _():
        for k in range(CHUNKS // 2, CHUNKS):
            for way in (1, -1):
                own_visits(way, k, start)
    forward_far(0)
    gift_afar(2)
    take_along(0)
    forward_far(1)
    take_along(1)
    forward_far(2)
    take_across(last)
    forward_far(last)
    take_along(2)
    for distance in range(3, outer - 1):
        for k in range(CHUNKS):
            forward(distance, k)
        gift_afar(distance)

    def meet(index):
        for layer in (index, outer - 1 - index):
            settle(layer, 1)

            @pl.when(visits_me(layer, 1))
            def _(layer=layer):
                prepare_rows(1, layer, visitors[1, slot(layer)])
        pair(1, 2 * index, 2, x, True)

    for step in range(1, outer):
        layer = lax.rem(z + step, outer)
        settle(layer, 0)
        prepare_rows(0, layer, visitors[0, slot(layer)])
    pair(0, 0, outer, x, True)

    @pl.when(place > 0)
    def _():
        meet(0)
    for k in range(CHUNKS):
        take_shared(k)
        if k == CHUNKS // 2 - 1:
            others(lambda step, column: prepare_columns(0, column))
    others(lambda step, column: prepare_columns(1, column))
    others(lambda step, column: pair(0, 0, outer, column, False))
    for step in range(1, outer):
        back(lax.rem(z + step, outer), 0).start()

    @pl.when(place == 0)
    def _():
        meet(0)
    for index in range(half):
        def finish(index=index):
            if index > 0:
                meet(index)
            others(lambda step, column: pair(1, 2 * index, 2, column, False))
            for layer in (index, outer - 1 - index):
                @pl.when(layer != z)
                def _(layer=layer):
                    back(layer, 1).start()

        if index == 0:
            finish()
        else:
            pl.when(place >= index)(finish)
        if index < half - 1:
            @pl.when(place > index)
            def _(index=index):
                outward(index)

            @pl.when(place == index + 1)
            def _():
                for step in range(1, inner * teams):
                    scatter(step).start()


    for way in (1, -1):
        for k in range(CHUNKS):
            own_visits(way, k, wait_send)
            for distance in range(1, outer - 1):
                layer = z - way * distance

                @pl.when(goes_on(layer, way, k))
                def _(way=way, k=k, layer=layer):
                    visit(layer, way, k, False, wait_send)
    for distance in range(1, outer - 1):
        gift(distance, wait_send)

    def sent(step, column):
        for k in range(CHUNKS):
            for copy in across(step, k):
                copy.wait_send()
            for other in range(planes):
                if other > 0 and k < CHUNKS - 1:
                    along(step, k, other).wait_send()
                share(step, k, other).wait_send()
    others(sent)


    mine = slot(z)
    for part in range(2):
        result = sums[part, mine]
        if part == 0:
            for step in range(1, outer):
                layer = lax.rem(z + step, outer)
                wait_recv(returned.at[0, slot(layer)], back_recv.at[0, layer])
                result = result + returned[0, slot(layer)]
            out_ref[0] = result
        else:
            out_ref[1] = result
            for step in range(1, outer):
                layer = lax.rem(z + step, outer)

                @pl.when(i_visit(layer, 1))
                def _(layer=layer):
                    wait_recv(returned.at[1, slot(layer)], back_recv.at[1, layer])
                    out_ref[1] = out_ref[1] + returned[1, slot(layer)]

            @pl.when(place > 0)
            def _():
                own = x * teams + team
                total = out_ref[1] + partial[x, team]
                for step in range(1, inner * teams):
                    index = lax.rem(own + step, inner * teams)
                    wait_recv(scattered.at[index], part_recv.at[index])
                    total = total + scattered[index]
                out_ref[1] = total
                for step in range(1, inner * teams):
                    scatter(step).wait_send()
    for step in range(1, outer):
        layer = lax.rem(z + step, outer)
        for part in range(2):
            @pl.when(visits_me(layer, part))
            def _(layer=layer, part=part):
                back(layer, part).wait_send()


def body(points, probes):
    rows, width = points.shape
    count = probes.shape[1]
    blocks, teams = lax.axis_size("blk"), lax.axis_size("team")
    inner = 1 << ((blocks.bit_length() - 1) // 2)
    outer = blocks // inner
    sub = rows // teams // 2
    every = width + count
    f32, bf16 = jnp.float32, jnp.bfloat16
    dma = pltpu.SemaphoreType.DMA
    planes = teams // CORES
    result = pl.pallas_call(
        functools.partial(kernel, outer, inner, teams),
        out_shape=jax.ShapeDtypeStruct((2, sub, count), f32),
        in_specs=[pl.BlockSpec(memory_space=pl.ANY)] * 2,
        out_specs=pl.BlockSpec(memory_space=pltpu.VMEM),
        scratch_shapes=[
            pltpu.VMEM((2, inner, teams, sub, every), f32),
            pltpu.VMEM((2, outer, sub, width), f32),
            pltpu.VMEM((2, outer, sub, count), f32),
            pltpu.VMEM((inner, 2 * teams * sub, width), bf16),
            pltpu.VMEM((inner, 2 * teams * sub, width), bf16),
            pltpu.VMEM((inner, 2 * teams * sub, count), bf16),
            pltpu.VMEM((inner, 2 * teams * sub, count), bf16),
            pltpu.VMEM((inner, 1, 2 * teams * sub), f32),
            pltpu.VMEM((2, 2, outer * sub, width), bf16),
            pltpu.VMEM((2, outer * sub, 1), f32),
            pltpu.VMEM((2, outer * sub, inner * teams * sub), f32),
            pltpu.VMEM((2, outer, sub, count), f32),
            pltpu.VMEM((2, outer, sub, count), f32),
            pltpu.VMEM((inner, teams, sub, count), f32),
            pltpu.VMEM((inner * teams, sub, count), f32),
            dma((2, 2)),
            dma((outer, 2, CHUNKS)),
            dma((outer, CHUNKS)),
            dma((outer,)),
            dma((outer,)),
            dma((inner - 1, CHUNKS + planes - 1)),
            dma((inner - 1, planes - 1, CHUNKS)),
            dma((inner - 1, planes, CHUNKS)),
            dma((inner, teams, CHUNKS)),
            dma((2, outer)),
            dma((2, outer)),
            dma((inner * teams,)),
            dma((inner * teams,)),
        ],
        compiler_params=pltpu.CompilerParams(
            collective_id=0, has_side_effects=True, vmem_limit_bytes=55100 * 2**10
        ),
    )(points.reshape(teams, 2, sub, width), probes.reshape(teams, 2, sub, count))
    return result.reshape(2 * sub, count)


def solution(mesh):
    in_specs = (P("blk", None), P("blk", None))
    out_specs = P(("blk", "team"), None)
    return jax.shard_map(body, mesh=mesh, in_specs=in_specs, out_specs=out_specs, check_vma=False)
```

```python
import functools

import jax
import jax.numpy as jnp
from jax import lax
from jax.experimental import pallas as pl
from jax.experimental.pallas import tpu as pltpu
from jax.sharding import PartitionSpec as P

MESH = pl.DeviceIdType.MESH
CHUNKS = 4
LEAPS = 1
CORES = 2


def kernel(
    outer,
    inner,
    teams,
    points_hbm,
    probes_hbm,
    out_ref,
    layer_all,
    visitors,
    visitor_vals,
    cols_high,
    cols_low,
    vals_high,
    vals_low,
    layer_sq,
    terms,
    visitor_sq,
    second,
    sums,
    returned,
    partial,
    scattered,
    load_sem,
    visit_send,
    visit_recv,
    leap_send,
    ready,
    gift_send,
    gift_recv,
    row_send,
    plane_send,
    share_send,
    row_recv,
    back_send,
    back_recv,
    part_send,
    part_recv,
):
    sub, count = sums.shape[2:]
    width = layer_all.shape[-1] - count
    every = width + count
    half = outer // 2
    planes = teams // CORES
    wide = teams * sub
    step_rows = 2 * sub // CHUNKS
    scale = 2.0 / width
    block = lax.axis_index("blk")
    team = lax.axis_index("team")
    z = block // inner
    x = lax.rem(block, inner)
    plane = team // CORES
    core = lax.rem(team, CORES)
    left = z < half
    near = jnp.where(left, 1, -1)
    place = jnp.where(left, z, outer - 1 - z)

    def at(layer, column, member=None):
        target = {"blk": layer * inner + column}
        if member is not None:
            target["team"] = member
        return target

    def slot(layer):
        return jnp.where(layer < half, 2 * layer, 2 * (outer - 1 - layer) + 1)

    def inside(layer):
        return layer * (outer - 1 - layer) >= 0

    def remote(src, dst, send, recv, target):
        return pltpu.make_async_remote_copy(
            src_ref=src, dst_ref=dst, send_sem=send, recv_sem=recv, device_id=target, device_id_type=MESH
        )

    def wait_recv(ref, sem):
        pltpu.make_async_copy(ref, ref, sem).wait()

    def chunk(k):
        return (k * 2) // CHUNKS, pl.ds((k % (CHUNKS // 2)) * step_rows, step_rows)


    def same_side(layer, way):
        return (layer < half) if way == 1 else (layer >= half)

    def visit(layer, way, k, first, op):
        part, rows = chunk(k)
        dst = visitors.at[part, slot(layer), rows]

        op(remote(
            layer_all.at[part, x, team, rows, pl.ds(0, width)] if first else dst,
            dst,
            visit_send.at[layer, (way + 1) // 2, k],
            visit_recv.at[layer, k],
            at(z + way, x),
        ))

    def start(copy):
        copy.start()

    def wait_send(copy):
        copy.wait_send()

    last = CHUNKS - 1

    def rank(layer):
        return jnp.minimum(layer, outer - 1 - layer)

    def is_end(layer):
        return rank(layer) == 0

    def own_visits(way, k, op):
        first, final = (0, outer - 2) if way == 1 else (1, outer - 1)
        if k >= CHUNKS // 2:
            first, final = (0, half - 1) if way == 1 else (half, outer - 1)

        @pl.when((z - first) * (final - z) >= 0)
        def _():
            visit(z, way, k, True, op)

    def leaps(k, op):
        part, rows = chunk(k)

        @pl.when((place == 0) & (outer > 3))
        def _():
            op(remote(
                layer_all.at[part, x, team, rows, pl.ds(0, width)],
                visitors.at[part, slot(z), rows],
                leap_send.at[k],
                visit_recv.at[z, k],
                at(z + 2 * near, x),
            ))

    def goes_on(layer, way, k):
        low, high = (0, outer - 2) if way == 1 else (1, outer - 1)
        first, final = 0, outer - 1
        if k < CHUNKS // 2:
            room = (z - low) * (high - z)
        else:
            first, final = (0, half - 1) if way == 1 else (half, outer - 1)
            room = outer - 1 - layer - (z + way) if way == 1 else layer + (z + way) - (outer - 1)
        leapt = layer + z - 2 if way == 1 else 2 * outer - 4 - layer - z
        if k < LEAPS or outer < 4:
            leapt = 0
        return jnp.minimum(jnp.minimum((layer - first) * (final - layer), room), leapt) >= 0

    def wait_visit(layer, k):
        part, rows = chunk(k)
        wait_recv(visitors.at[part, slot(layer), rows], visit_recv.at[layer, k])

    def forward(distance, k):
        for way in (1, -1):
            layer = z - way * distance

            @pl.when(goes_on(layer, way, k))
            def _(way=way, layer=layer):
                wait_visit(layer, k)
                visit(layer, way, k, False, start)

    def asked(distance):
        return (place == 0) & (distance > 2) & (distance < outer - 1)

    def settle(layer, part):
        for k in range(part * CHUNKS // 2, (part + 1) * CHUNKS // 2):
            for way in (1, -1):
                ahead = way * (z - layer) > 0
                stays = ahead & jnp.logical_not(goes_on(layer, way, k))
                if part == 1:
                    stays = stays & (rank(layer) <= place)
                if k == 0:
                    stays = stays & jnp.logical_not(asked(way * (z - layer)))

                @pl.when(stays)
                def _(k=k):
                    wait_visit(layer, k)

    def gift(distance, op, ends=None):
        room = outer - 2 - 2 * place - distance
        if ends is not None:
            room = jnp.minimum(room, -place if ends else place - 1)

        @pl.when(room >= 0)
        def _():
            op(remote(
                layer_all.at[:, x, team, :, pl.ds(width, count)],
                visitor_vals.at[:, slot(z)],
                gift_send.at[distance],
                gift_recv.at[z],
                at(z + near * distance, x),
            ))

    def gift_afar(distance):
        if distance < outer - 1:
            @pl.when(place == 0)
            def _():
                wait_visit(z + near * distance, 0)
            gift(distance, start)


    def piece(column, member, k):
        part, rows = chunk(k)
        return layer_all.at[part, column, member, rows]

    def arrives(k, other):
        return k == CHUNKS - 1 or other == 0

    def member_of(other):
        return lax.rem(plane + other, planes) * CORES + core

    def across(step, k):
        return [
            remote(
                piece(x, member_of(other), k),
                piece(x, member_of(other), k),
                row_send.at[step - 1, k + other],
                row_recv.at[x, member_of(other), k],
                at(z, lax.rem(x + step, inner)),
            )
            for other in range(planes)
            if arrives(k, other)
        ]

    def along(step, k, other):
        column = lax.rem(x + step, inner)
        return remote(
            piece(column, team, k),
            piece(column, team, k),
            plane_send.at[step - 1, other - 1, k],
            row_recv.at[column, team, k],
            at(z, x, member_of(other)),
        )

    def share(step, k, other):
        column = lax.rem(x + step, inner)
        return remote(
            piece(column, member_of(other), k),
            piece(column, member_of(other), k),
            share_send.at[step - 1, other, k],
            row_recv.at[column, member_of(other), k],
            at(z, x, team + 1 - 2 * core),
        )

    def others(work):
        if inner == 2:
            work(1, 1 - x)
            return

        def one(step, carry):
            work(step, lax.rem(x + step, inner))
            return carry
        lax.fori_loop(1, inner, one, 0)

    def wait_piece(column, member, k):
        wait_recv(piece(column, member, k), row_recv.at[column, member, k])

    def take_across(k):
        def take(step, column):
            for other in range(planes):
                if arrives(k, other):
                    wait_piece(column, member_of(other), k)
                    if k < CHUNKS - 1:
                        for further in range(1, planes):
                            along(step, k, further).start()
                    share(step, k, other).start()
        others(take)

    def take_along(k):
        def take(step, column):
            for other in range(1, planes):
                wait_piece(column, member_of(other), k)
                share(step, k, other).start()
        others(take)

    def take_shared(k):
        def take(step, column):
            for other in range(planes):
                wait_piece(column, member_of(other) + 1 - 2 * core, k)
        others(take)


    def back(layer, part):
        return remote(
            sums.at[part, slot(layer)],
            returned.at[part, slot(z)],
            back_send.at[part, layer],
            back_recv.at[part, z],
            at(layer, x),
        )

    def visits_me(layer, part):
        if part == 0:
            return layer != z
        return (layer != z) & (rank(layer) <= place)

    def i_visit(layer, part):
        if part == 0:
            return layer != z
        return (layer != z) & (place <= rank(layer))

    def scatter(step):
        index = lax.rem(x * teams + team + step, inner * teams)
        return remote(
            partial.at[index // teams, lax.rem(index, teams)],
            scattered.at[x * teams + team],
            part_send.at[index],
            part_recv.at[x * teams + team],
            at(z, index // teams, lax.rem(index, teams)),
        )


    def two_terms(values):
        high = values.astype(jnp.bfloat16)
        return high, (values - high.astype(jnp.float32)).astype(jnp.bfloat16)

    def four_products(stacked, high, low, contract):
        rows = stacked.shape[0] // 2
        dot = functools.partial(
            lax.dot_general,
            dimension_numbers=(contract, ((), ())),
            preferred_element_type=jnp.float32,
        )
        by_high, by_low = dot(stacked, high), dot(stacked, low)
        return by_high[:rows] + (by_high[rows:] + by_low[:rows] + by_low[rows:])

    def prepare_columns(part, column):
        where = slice(part * wide, (part + 1) * wide)
        values = layer_all[part, column, :, :, 0:width].reshape(wide, width)
        total = jnp.sum(values * values, axis=1, keepdims=True)
        layer_sq[column, :, where] = jnp.broadcast_to(total, (wide, 128)).T[0:1, :]
        cols_high[column, where], cols_low[column, where] = two_terms(values)
        rest = layer_all[part, column, :, :, width:every].reshape(wide, count)
        vals_high[column, where], vals_low[column, where] = two_terms(rest)

    def prepare_rows(part, layer, values):
        where = pl.ds(pl.multiple_of(slot(layer) * sub, sub), sub)
        visitor_sq[part, where] = jnp.sum(values * values, axis=1, keepdims=True)
        high, low = two_terms(values)
        terms[part, 0, where, :] = high
        terms[part, 1, where, :] = low

    def pair(part, begin, size, column, fresh):
        rows = slice(begin * sub, (begin + size) * sub)
        cross = four_products(
            terms[part, :, rows, :].reshape(2 * size * sub, width),
            cols_high[column],
            cols_low[column],
            ((1,), (1,)),
        )
        arg = (visitor_sq[part, rows] + layer_sq[column] - 2.0 * cross) * scale
        value = jnp.exp(-jnp.maximum(arg, 0.0))
        second[part, rows, pl.ds(pl.multiple_of(column * wide, wide), wide)] = value[:, wide:]
        product = four_products(
            jnp.concatenate(two_terms(value), axis=0), vals_high[column], vals_low[column], ((1,), (0,))
        ).reshape(size, sub, count)
        kept = slice(begin, begin + size)
        sums[part, kept] = product if fresh else sums[part, kept] + product

    def outward(index):
        for layer in (index, outer - 1 - index):
            wait_recv(visitor_vals.at[:, slot(layer)], gift_recv.at[layer])
        rows = slice(2 * index * sub, 2 * (index + 1) * sub)
        value = jnp.concatenate([second[0, rows, :], second[1, rows, :]], axis=0).T
        rest = visitor_vals[:, 2 * index : 2 * (index + 1)].reshape(4 * sub, count)
        high, low = two_terms(rest)
        product = four_products(jnp.concatenate(two_terms(value), axis=0), high, low, ((1,), (0,)))
        product = product.reshape(inner, teams, sub, count)
        partial[...] = product if index == 0 else partial[...] + product


    loads = [
        pltpu.make_async_copy(
            source.at[:, part], layer_all.at[part, x, :, :, pl.ds(begin, extent)], load_sem.at[part, which]
        )
        for part in range(2)
        for which, (source, begin, extent) in enumerate(((points_hbm, 0, width), (probes_hbm, width, count)))
    ]
    barrier = pltpu.get_barrier_semaphore()

    def greet(target):
        pl.semaphore_signal(barrier, inc=1, device_id=target, device_id_type=MESH)

    for way in (1, -1):
        @pl.when(inside(z + way))
        def _(way=way):
            greet(at(z + way, x))
    for step in range(1, inner):
        greet(at(z, lax.rem(x + step, inner)))
    for other in range(1, planes):
        greet(at(z, x, member_of(other)))
    greet(at(z, x, team + 1 - 2 * core))
    for load in loads:
        load.start()
    for load in loads:
        load.wait()
    pl.semaphore_wait(barrier, jnp.where(is_end(z), 1, 2) + inner - 1 + planes)

    if outer > 3:
        @pl.when(place == 1)
        def _():
            pl.semaphore_signal(ready, inc=1, device_id=at(z - near, x), device_id_type=MESH)


    for k in range(CHUNKS):
        if k < CHUNKS // 2:
            for way in (1, -1):
                own_visits(way, k, start)
        for step in range(1, inner):
            for copy in across(step, k):
                copy.start()

    for part in range(2):
        prepare_columns(part, x)
        prepare_rows(part, z, layer_all[part, x, team, :, 0:width])

    if outer > 3:
        @pl.when(place == 0)
        def _():
            pl.semaphore_wait(ready, 1)
    for k in range(LEAPS, CHUNKS):
        leaps(k, start)
    for k in range(CHUNKS // 2, CHUNKS):
        for way in (1, -1):
            @pl.when(place == 0)
            def _(way=way, k=k):
                own_visits(way, k, start)
    gift(1, start)
    gift(2, start, True)

    def forward_far(k):
        if outer > 3:
            forward(2, k)

    def own_second():
        @pl.when(place > 0)
        def _():
            for k in range(CHUNKS // 2, CHUNKS):
                for way in (1, -1):
                    own_visits(way, k, start)

    for k in range(last):
        forward(1, k)
        take_across(k)
        if k == 0:
            own_second()
    forward(1, last)

    forward_far(1)
    forward_far(0)
    gift(2, start, False)
    forward_far(2)
    take_along(0)
    forward_far(last)
    for distance in range(3, outer - 1):
        for k in range(CHUNKS):
            forward(distance, k)
        gift_afar(distance)

    def meet_first():
        for step in range(1, outer):
            layer = lax.rem(z + step, outer)
            settle(layer, 0)
            prepare_rows(0, layer, visitors[0, slot(layer)])
        pair(0, 0, outer, x, True)

    def meet(index):
        for layer in (index, outer - 1 - index):
            settle(layer, 1)

            @pl.when(visits_me(layer, 1))
            def _(layer=layer):
                prepare_rows(1, layer, visitors[1, slot(layer)])
        pair(1, 2 * index, 2, x, True)

    @pl.when(place > 0)
    def _():
        meet_first()
    take_along(1)
    take_across(last)
    take_along(2)
    @pl.when(place == 0)
    def _():
        meet_first()
    take_shared(0)
    take_shared(1)
    others(lambda step, column: prepare_columns(0, column))

    take_shared(2)
    take_shared(last)
    others(lambda step, column: prepare_columns(1, column))

    others(lambda step, column: pair(0, 0, outer, column, False))
    for distance in range(outer - 1, 0, -1):
        for way in (1, -1):
            @pl.when(inside(z + way * distance))
            def _(layer=z + way * distance):
                back(layer, 0).start()

    meet(0)
    for index in range(half):
        def finish(index=index):
            if index > 0:
                meet(index)
            others(lambda step, column: pair(1, 2 * index, 2, column, False))
            for layer in (index, outer - 1 - index):
                @pl.when(layer != z)
                def _(layer=layer):
                    back(layer, 1).start()

        if index == 0:
            finish()
        else:
            pl.when(place >= index)(finish)
        if index < half - 1:
            @pl.when(place > index)
            def _(index=index):
                outward(index)

            @pl.when(place == index + 1)
            def _():
                for step in range(1, inner * teams):
                    scatter(step).start()


    for k in range(LEAPS, CHUNKS):
        leaps(k, wait_send)
    for way in (1, -1):
        for k in range(CHUNKS):
            own_visits(way, k, wait_send)
            for distance in range(1, outer - 1):
                layer = z - way * distance

                @pl.when(goes_on(layer, way, k))
                def _(way=way, k=k, layer=layer):
                    visit(layer, way, k, False, wait_send)
    for distance in range(1, outer - 1):
        gift(distance, wait_send)

    def sent(step, column):
        for k in range(CHUNKS):
            for copy in across(step, k):
                copy.wait_send()
            for other in range(planes):
                if other > 0 and k < CHUNKS - 1:
                    along(step, k, other).wait_send()
                share(step, k, other).wait_send()
    others(sent)


    mine = slot(z)
    for part in range(2):
        result = sums[part, mine]
        if part == 0:
            for step in range(1, outer):
                layer = lax.rem(z + step, outer)
                wait_recv(returned.at[0, slot(layer)], back_recv.at[0, layer])
                result = result + returned[0, slot(layer)]
            out_ref[0] = result
        else:
            out_ref[1] = result
            for step in range(1, outer):
                layer = lax.rem(z + step, outer)

                @pl.when(i_visit(layer, 1))
                def _(layer=layer):
                    wait_recv(returned.at[1, slot(layer)], back_recv.at[1, layer])
                    out_ref[1] = out_ref[1] + returned[1, slot(layer)]

            @pl.when(place > 0)
            def _():
                own = x * teams + team
                total = out_ref[1] + partial[x, team]
                for step in range(1, inner * teams):
                    index = lax.rem(own + step, inner * teams)
                    wait_recv(scattered.at[index], part_recv.at[index])
                    total = total + scattered[index]
                out_ref[1] = total
                for step in range(1, inner * teams):
                    scatter(step).wait_send()
    for step in range(1, outer):
        layer = lax.rem(z + step, outer)
        for part in range(2):
            @pl.when(visits_me(layer, part))
            def _(layer=layer, part=part):
                back(layer, part).wait_send()


def body(points, probes):
    rows, width = points.shape
    count = probes.shape[1]
    blocks, teams = lax.axis_size("blk"), lax.axis_size("team")
    inner = 1 << ((blocks.bit_length() - 1) // 2)
    outer = blocks // inner
    sub = rows // teams // 2
    every = width + count
    f32, bf16 = jnp.float32, jnp.bfloat16
    dma = pltpu.SemaphoreType.DMA
    planes = teams // CORES
    result = pl.pallas_call(
        functools.partial(kernel, outer, inner, teams),
        out_shape=jax.ShapeDtypeStruct((2, sub, count), f32),
        in_specs=[pl.BlockSpec(memory_space=pl.ANY)] * 2,
        out_specs=pl.BlockSpec(memory_space=pltpu.VMEM),
        scratch_shapes=[
            pltpu.VMEM((2, inner, teams, sub, every), f32),
            pltpu.VMEM((2, outer, sub, width), f32),
            pltpu.VMEM((2, outer, sub, count), f32),
            pltpu.VMEM((inner, 2 * teams * sub, width), bf16),
            pltpu.VMEM((inner, 2 * teams * sub, width), bf16),
            pltpu.VMEM((inner, 2 * teams * sub, count), bf16),
            pltpu.VMEM((inner, 2 * teams * sub, count), bf16),
            pltpu.VMEM((inner, 1, 2 * teams * sub), f32),
            pltpu.VMEM((2, 2, outer * sub, width), bf16),
            pltpu.VMEM((2, outer * sub, 1), f32),
            pltpu.VMEM((2, outer * sub, inner * teams * sub), f32),
            pltpu.VMEM((2, outer, sub, count), f32),
            pltpu.VMEM((2, outer, sub, count), f32),
            pltpu.VMEM((inner, teams, sub, count), f32),
            pltpu.VMEM((inner * teams, sub, count), f32),
            dma((2, 2)),
            dma((outer, 2, CHUNKS)),
            dma((outer, CHUNKS)),
            dma((CHUNKS,)),
            pltpu.SemaphoreType.REGULAR,
            dma((outer,)),
            dma((outer,)),
            dma((inner - 1, CHUNKS + planes - 1)),
            dma((inner - 1, planes - 1, CHUNKS)),
            dma((inner - 1, planes, CHUNKS)),
            dma((inner, teams, CHUNKS)),
            dma((2, outer)),
            dma((2, outer)),
            dma((inner * teams,)),
            dma((inner * teams,)),
        ],
        compiler_params=pltpu.CompilerParams(
            collective_id=0, has_side_effects=True, vmem_limit_bytes=55100 * 2**10
        ),
    )(points.reshape(teams, 2, sub, width), probes.reshape(teams, 2, sub, count))
    return result.reshape(2 * sub, count)


def solution(mesh):
    in_specs = (P("blk", None), P("blk", None))
    out_specs = P(("blk", "team"), None)
    return jax.shard_map(body, mesh=mesh, in_specs=in_specs, out_specs=out_specs, check_vma=False)
```

```python
import functools

import jax
import jax.numpy as jnp
from jax import lax
from jax.experimental import pallas as pl
from jax.experimental.pallas import tpu as pltpu
from jax.sharding import PartitionSpec as P

MESH = pl.DeviceIdType.MESH
CHUNKS = 4
LEAPS = 1
CORES = 2


def kernel(
    outer,
    inner,
    teams,
    points_hbm,
    probes_hbm,
    out_ref,
    layer_all,
    visitors,
    visitor_vals,
    cols_high,
    cols_low,
    vals_high,
    vals_low,
    layer_sq,
    terms,
    visitor_sq,
    second,
    sums,
    returned,
    partial,
    scattered,
    load_sem,
    visit_send,
    visit_recv,
    leap_send,
    ready,
    gift_send,
    gift_recv,
    row_send,
    plane_send,
    share_send,
    row_recv,
    back_send,
    back_recv,
    part_send,
    part_recv,
):
    sub, count = sums.shape[2:]
    width = layer_all.shape[-1] - count
    every = width + count
    half = outer // 2
    planes = teams // CORES
    wide = teams * sub
    step_rows = 2 * sub // CHUNKS
    scale = 2.0 / width
    block = lax.axis_index("blk")
    team = lax.axis_index("team")
    z = block // inner
    x = lax.rem(block, inner)
    plane = team // CORES
    core = lax.rem(team, CORES)
    left = z < half
    near = jnp.where(left, 1, -1)
    place = jnp.where(left, z, outer - 1 - z)

    def at(layer, column, member=None):
        target = {"blk": layer * inner + column}
        if member is not None:
            target["team"] = member
        return target

    def slot(layer):
        return jnp.where(layer < half, 2 * layer, 2 * (outer - 1 - layer) + 1)

    def inside(layer):
        return layer * (outer - 1 - layer) >= 0

    def remote(src, dst, send, recv, target):
        return pltpu.make_async_remote_copy(
            src_ref=src, dst_ref=dst, send_sem=send, recv_sem=recv, device_id=target, device_id_type=MESH
        )

    def wait_recv(ref, sem):
        pltpu.make_async_copy(ref, ref, sem).wait()

    def chunk(k):
        return (k * 2) // CHUNKS, pl.ds((k % (CHUNKS // 2)) * step_rows, step_rows)


    def same_side(layer, way):
        return (layer < half) if way == 1 else (layer >= half)

    def visit(layer, way, k, first, op):
        part, rows = chunk(k)
        dst = visitors.at[part, slot(layer), rows]

        op(remote(
            layer_all.at[part, x, team, rows, pl.ds(0, width)] if first else dst,
            dst,
            visit_send.at[layer, (way + 1) // 2, k],
            visit_recv.at[layer, k],
            at(z + way, x),
        ))

    def start(copy):
        copy.start()

    def wait_send(copy):
        copy.wait_send()

    last = CHUNKS - 1

    def rank(layer):
        return jnp.minimum(layer, outer - 1 - layer)

    def is_end(layer):
        return rank(layer) == 0

    def own_visits(way, k, op):
        first, final = (0, outer - 2) if way == 1 else (1, outer - 1)
        if k >= CHUNKS // 2:
            first, final = (0, half - 1) if way == 1 else (half, outer - 1)

        @pl.when((z - first) * (final - z) >= 0)
        def _():
            visit(z, way, k, True, op)

    def leaps(k, op):
        part, rows = chunk(k)

        @pl.when((place == 0) & (outer > 3))
        def _():
            op(remote(
                layer_all.at[part, x, team, rows, pl.ds(0, width)],
                visitors.at[part, slot(z), rows],
                leap_send.at[k],
                visit_recv.at[z, k],
                at(z + 2 * near, x),
            ))

    def goes_on(layer, way, k):
        low, high = (0, outer - 2) if way == 1 else (1, outer - 1)
        first, final = 0, outer - 1
        if k < CHUNKS // 2:
            room = (z - low) * (high - z)
        else:
            first, final = (0, half - 1) if way == 1 else (half, outer - 1)
            room = outer - 1 - layer - (z + way) if way == 1 else layer + (z + way) - (outer - 1)
        leapt = layer + z - 2 if way == 1 else 2 * outer - 4 - layer - z
        if k < LEAPS or outer < 4:
            leapt = 0
        return jnp.minimum(jnp.minimum((layer - first) * (final - layer), room), leapt) >= 0

    def wait_visit(layer, k):
        part, rows = chunk(k)
        wait_recv(visitors.at[part, slot(layer), rows], visit_recv.at[layer, k])

    def forward(distance, k):
        for way in (1, -1):
            layer = z - way * distance

            @pl.when(goes_on(layer, way, k))
            def _(way=way, layer=layer):
                wait_visit(layer, k)
                visit(layer, way, k, False, start)

    def asked(distance):
        return (place == 0) & (distance > 2) & (distance < outer - 1)

    def settle(layer, part):
        for k in range(part * CHUNKS // 2, (part + 1) * CHUNKS // 2):
            for way in (1, -1):
                ahead = way * (z - layer) > 0
                stays = ahead & jnp.logical_not(goes_on(layer, way, k))
                if part == 1:
                    stays = stays & (rank(layer) <= place)
                if k == 0:
                    stays = stays & jnp.logical_not(asked(way * (z - layer)))

                @pl.when(stays)
                def _(k=k):
                    wait_visit(layer, k)

    def gift(distance, op, ends=None):
        room = outer - 2 - 2 * place - distance
        if ends is not None:
            room = jnp.minimum(room, -place if ends else place - 1)

        @pl.when(room >= 0)
        def _():
            op(remote(
                layer_all.at[:, x, team, :, pl.ds(width, count)],
                visitor_vals.at[:, slot(z)],
                gift_send.at[distance],
                gift_recv.at[z],
                at(z + near * distance, x),
            ))

    def gift_afar(distance):
        if distance < outer - 1:
            @pl.when(place == 0)
            def _():
                wait_visit(z + near * distance, 0)
            gift(distance, start)


    def piece(column, member, k):
        begin, size = ((0, sub // 2), (sub // 2, sub // 2), (0, sub // 4), (sub // 4, 3 * sub // 4))[k]
        return layer_all.at[k // (CHUNKS // 2), column, member, pl.ds(begin, size)]

    def arrives(k, other):
        return k == CHUNKS - 1 or other == 0

    def member_of(other):
        return lax.rem(plane + other, planes) * CORES + core

    def across(step, k):
        return [
            remote(
                piece(x, member_of(other), k),
                piece(x, member_of(other), k),
                row_send.at[step - 1, k + other],
                row_recv.at[x, member_of(other), k],
                at(z, lax.rem(x + step, inner)),
            )
            for other in range(planes)
            if arrives(k, other)
        ]

    def along(step, k, other):
        column = lax.rem(x + step, inner)
        return remote(
            piece(column, team, k),
            piece(column, team, k),
            plane_send.at[step - 1, other - 1, k],
            row_recv.at[column, team, k],
            at(z, x, member_of(other)),
        )

    def share(step, k, other):
        column = lax.rem(x + step, inner)
        return remote(
            piece(column, member_of(other), k),
            piece(column, member_of(other), k),
            share_send.at[step - 1, other, k],
            row_recv.at[column, member_of(other), k],
            at(z, x, team + 1 - 2 * core),
        )

    def others(work):
        if inner == 2:
            work(1, 1 - x)
            return

        def one(step, carry):
            work(step, lax.rem(x + step, inner))
            return carry
        lax.fori_loop(1, inner, one, 0)

    def wait_piece(column, member, k):
        wait_recv(piece(column, member, k), row_recv.at[column, member, k])

    def take_across(k):
        def take(step, column):
            for other in range(planes):
                if arrives(k, other):
                    wait_piece(column, member_of(other), k)
                    if k < CHUNKS - 1:
                        for further in range(1, planes):
                            along(step, k, further).start()
                    share(step, k, other).start()
        others(take)

    def take_along(k):
        def take(step, column):
            for other in range(1, planes):
                wait_piece(column, member_of(other), k)
                share(step, k, other).start()
        others(take)

    def take_shared(k):
        def take(step, column):
            for other in range(planes):
                wait_piece(column, member_of(other) + 1 - 2 * core, k)
        others(take)


    def back(layer, part):
        return remote(
            sums.at[part, slot(layer)],
            returned.at[part, slot(z)],
            back_send.at[part, layer],
            back_recv.at[part, z],
            at(layer, x),
        )

    def visits_me(layer, part):
        if part == 0:
            return layer != z
        return (layer != z) & (rank(layer) <= place)

    def i_visit(layer, part):
        if part == 0:
            return layer != z
        return (layer != z) & (place <= rank(layer))

    def scatter(step):
        index = lax.rem(x * teams + team + step, inner * teams)
        return remote(
            partial.at[index // teams, lax.rem(index, teams)],
            scattered.at[x * teams + team],
            part_send.at[index],
            part_recv.at[x * teams + team],
            at(z, index // teams, lax.rem(index, teams)),
        )


    def two_terms(values):
        high = values.astype(jnp.bfloat16)
        return high, (values - high.astype(jnp.float32)).astype(jnp.bfloat16)

    def four_products(stacked, high, low, contract):
        rows = stacked.shape[0] // 2
        dot = functools.partial(
            lax.dot_general,
            dimension_numbers=(contract, ((), ())),
            preferred_element_type=jnp.float32,
        )
        by_high, by_low = dot(stacked, high), dot(stacked, low)
        return by_high[:rows] + (by_high[rows:] + by_low[:rows] + by_low[rows:])

    def prepare_columns(part, column):
        where = slice(part * wide, (part + 1) * wide)
        values = layer_all[part, column, :, :, 0:width].reshape(wide, width)
        total = jnp.sum(values * values, axis=1, keepdims=True)
        layer_sq[column, :, where] = jnp.broadcast_to(total, (wide, 128)).T[0:1, :]
        cols_high[column, where], cols_low[column, where] = two_terms(values)
        rest = layer_all[part, column, :, :, width:every].reshape(wide, count)
        vals_high[column, where], vals_low[column, where] = two_terms(rest)

    def prepare_rows(part, layer, values):
        where = pl.ds(pl.multiple_of(slot(layer) * sub, sub), sub)
        visitor_sq[part, where] = jnp.sum(values * values, axis=1, keepdims=True)
        high, low = two_terms(values)
        terms[part, 0, where, :] = high
        terms[part, 1, where, :] = low

    def pair(part, begin, size, column, fresh):
        rows = slice(begin * sub, (begin + size) * sub)
        cross = four_products(
            terms[part, :, rows, :].reshape(2 * size * sub, width),
            cols_high[column],
            cols_low[column],
            ((1,), (1,)),
        )
        arg = (visitor_sq[part, rows] + layer_sq[column] - 2.0 * cross) * scale
        value = jnp.exp(-jnp.maximum(arg, 0.0))
        second[part, rows, pl.ds(pl.multiple_of(column * wide, wide), wide)] = value[:, wide:]
        product = four_products(
            jnp.concatenate(two_terms(value), axis=0), vals_high[column], vals_low[column], ((1,), (0,))
        ).reshape(size, sub, count)
        kept = slice(begin, begin + size)
        sums[part, kept] = product if fresh else sums[part, kept] + product

    def outward(index):
        for layer in (index, outer - 1 - index):
            wait_recv(visitor_vals.at[:, slot(layer)], gift_recv.at[layer])
        rows = slice(2 * index * sub, 2 * (index + 1) * sub)
        value = jnp.concatenate([second[0, rows, :], second[1, rows, :]], axis=0).T
        rest = visitor_vals[:, 2 * index : 2 * (index + 1)].reshape(4 * sub, count)
        high, low = two_terms(rest)
        product = four_products(jnp.concatenate(two_terms(value), axis=0), high, low, ((1,), (0,)))
        product = product.reshape(inner, teams, sub, count)
        partial[...] = product if index == 0 else partial[...] + product


    loads = [
        pltpu.make_async_copy(
            source.at[:, part], layer_all.at[part, x, :, :, pl.ds(begin, extent)], load_sem.at[part, which]
        )
        for part in range(2)
        for which, (source, begin, extent) in enumerate(((points_hbm, 0, width), (probes_hbm, width, count)))
    ]
    barrier = pltpu.get_barrier_semaphore()

    def greet(target):
        pl.semaphore_signal(barrier, inc=1, device_id=target, device_id_type=MESH)

    for way in (1, -1):
        @pl.when(inside(z + way))
        def _(way=way):
            greet(at(z + way, x))
    for step in range(1, inner):
        greet(at(z, lax.rem(x + step, inner)))
    for other in range(1, planes):
        greet(at(z, x, member_of(other)))
    greet(at(z, x, team + 1 - 2 * core))
    for load in loads:
        load.start()
    for load in loads:
        load.wait()
    pl.semaphore_wait(barrier, jnp.where(is_end(z), 1, 2) + inner - 1 + planes)

    if outer > 3:
        @pl.when(place == 1)
        def _():
            pl.semaphore_signal(ready, inc=1, device_id=at(z - near, x), device_id_type=MESH)


    for k in range(CHUNKS):
        if k < CHUNKS // 2:
            for way in (1, -1):
                own_visits(way, k, start)
        for step in range(1, inner):
            for copy in across(step, k):
                copy.start()

    for part in range(2):
        prepare_columns(part, x)
        prepare_rows(part, z, layer_all[part, x, team, :, 0:width])

    if outer > 3:
        @pl.when(place == 0)
        def _():
            pl.semaphore_wait(ready, 1)
    for k in range(LEAPS, CHUNKS):
        leaps(k, start)
    for k in range(CHUNKS // 2, CHUNKS):
        for way in (1, -1):
            @pl.when(place == 0)
            def _(way=way, k=k):
                own_visits(way, k, start)
    gift(1, start)
    gift(2, start, True)

    def forward_far(k):
        if outer > 3:
            forward(2, k)

    def own_second():
        @pl.when(place > 0)
        def _():
            for k in range(CHUNKS // 2, CHUNKS):
                for way in (1, -1):
                    own_visits(way, k, start)

    for k in range(last):
        forward(1, k)
        take_across(k)
        if k == 0:
            own_second()
    forward(1, last)

    forward_far(1)
    forward_far(0)
    gift(2, start, False)
    forward_far(2)
    take_along(0)
    forward_far(last)
    for distance in range(3, outer - 1):
        for k in range(CHUNKS):
            forward(distance, k)
        gift_afar(distance)

    def meet_first():
        for step in range(1, outer):
            layer = lax.rem(z + step, outer)
            settle(layer, 0)
            prepare_rows(0, layer, visitors[0, slot(layer)])
        pair(0, 0, outer, x, True)

    def meet(index):
        for layer in (index, outer - 1 - index):
            settle(layer, 1)

            @pl.when(visits_me(layer, 1))
            def _(layer=layer):
                prepare_rows(1, layer, visitors[1, slot(layer)])
        pair(1, 2 * index, 2, x, True)

    @pl.when(place > 0)
    def _():
        meet_first()
    take_along(1)
    take_along(2)
    take_across(last)
    @pl.when(place == 0)
    def _():
        meet_first()
    take_shared(0)
    take_shared(1)
    others(lambda step, column: prepare_columns(0, column))

    take_shared(2)
    take_shared(last)
    others(lambda step, column: prepare_columns(1, column))

    others(lambda step, column: pair(0, 0, outer, column, False))
    for distance in range(outer - 1, 0, -1):
        for way in (1, -1):
            @pl.when(inside(z + way * distance))
            def _(layer=z + way * distance):
                back(layer, 0).start()

    meet(0)
    for index in range(half):
        def finish(index=index):
            if index > 0:
                meet(index)
            others(lambda step, column: pair(1, 2 * index, 2, column, False))
            for layer in (index, outer - 1 - index):
                @pl.when(layer != z)
                def _(layer=layer):
                    back(layer, 1).start()

        if index == 0:
            finish()
        else:
            pl.when(place >= index)(finish)
        if index < half - 1:
            @pl.when(place > index)
            def _(index=index):
                outward(index)

            @pl.when(place == index + 1)
            def _():
                for step in range(1, inner * teams):
                    scatter(step).start()


    for k in range(LEAPS, CHUNKS):
        leaps(k, wait_send)
    for way in (1, -1):
        for k in range(CHUNKS):
            own_visits(way, k, wait_send)
            for distance in range(1, outer - 1):
                layer = z - way * distance

                @pl.when(goes_on(layer, way, k))
                def _(way=way, k=k, layer=layer):
                    visit(layer, way, k, False, wait_send)
    for distance in range(1, outer - 1):
        gift(distance, wait_send)

    def sent(step, column):
        for k in range(CHUNKS):
            for copy in across(step, k):
                copy.wait_send()
            for other in range(planes):
                if other > 0 and k < CHUNKS - 1:
                    along(step, k, other).wait_send()
                share(step, k, other).wait_send()
    others(sent)


    mine = slot(z)
    for part in range(2):
        result = sums[part, mine]
        if part == 0:
            for step in range(1, outer):
                layer = lax.rem(z + step, outer)
                wait_recv(returned.at[0, slot(layer)], back_recv.at[0, layer])
                result = result + returned[0, slot(layer)]
            out_ref[0] = result
        else:
            out_ref[1] = result
            for step in range(1, outer):
                layer = lax.rem(z + step, outer)

                @pl.when(i_visit(layer, 1))
                def _(layer=layer):
                    wait_recv(returned.at[1, slot(layer)], back_recv.at[1, layer])
                    out_ref[1] = out_ref[1] + returned[1, slot(layer)]

            @pl.when(place > 0)
            def _():
                own = x * teams + team
                total = out_ref[1] + partial[x, team]
                for step in range(1, inner * teams):
                    index = lax.rem(own + step, inner * teams)
                    wait_recv(scattered.at[index], part_recv.at[index])
                    total = total + scattered[index]
                out_ref[1] = total
                for step in range(1, inner * teams):
                    scatter(step).wait_send()
    for step in range(1, outer):
        layer = lax.rem(z + step, outer)
        for part in range(2):
            @pl.when(visits_me(layer, part))
            def _(layer=layer, part=part):
                back(layer, part).wait_send()


def body(points, probes):
    rows, width = points.shape
    count = probes.shape[1]
    blocks, teams = lax.axis_size("blk"), lax.axis_size("team")
    inner = 1 << ((blocks.bit_length() - 1) // 2)
    outer = blocks // inner
    sub = rows // teams // 2
    every = width + count
    f32, bf16 = jnp.float32, jnp.bfloat16
    dma = pltpu.SemaphoreType.DMA
    planes = teams // CORES
    result = pl.pallas_call(
        functools.partial(kernel, outer, inner, teams),
        out_shape=jax.ShapeDtypeStruct((2, sub, count), f32),
        in_specs=[pl.BlockSpec(memory_space=pl.ANY)] * 2,
        out_specs=pl.BlockSpec(memory_space=pltpu.VMEM),
        scratch_shapes=[
            pltpu.VMEM((2, inner, teams, sub, every), f32),
            pltpu.VMEM((2, outer, sub, width), f32),
            pltpu.VMEM((2, outer, sub, count), f32),
            pltpu.VMEM((inner, 2 * teams * sub, width), bf16),
            pltpu.VMEM((inner, 2 * teams * sub, width), bf16),
            pltpu.VMEM((inner, 2 * teams * sub, count), bf16),
            pltpu.VMEM((inner, 2 * teams * sub, count), bf16),
            pltpu.VMEM((inner, 1, 2 * teams * sub), f32),
            pltpu.VMEM((2, 2, outer * sub, width), bf16),
            pltpu.VMEM((2, outer * sub, 1), f32),
            pltpu.VMEM((2, outer * sub, inner * teams * sub), f32),
            pltpu.VMEM((2, outer, sub, count), f32),
            pltpu.VMEM((2, outer, sub, count), f32),
            pltpu.VMEM((inner, teams, sub, count), f32),
            pltpu.VMEM((inner * teams, sub, count), f32),
            dma((2, 2)),
            dma((outer, 2, CHUNKS)),
            dma((outer, CHUNKS)),
            dma((CHUNKS,)),
            pltpu.SemaphoreType.REGULAR,
            dma((outer,)),
            dma((outer,)),
            dma((inner - 1, CHUNKS + planes - 1)),
            dma((inner - 1, planes - 1, CHUNKS)),
            dma((inner - 1, planes, CHUNKS)),
            dma((inner, teams, CHUNKS)),
            dma((2, outer)),
            dma((2, outer)),
            dma((inner * teams,)),
            dma((inner * teams,)),
        ],
        compiler_params=pltpu.CompilerParams(
            collective_id=0, has_side_effects=True, vmem_limit_bytes=55100 * 2**10
        ),
    )(points.reshape(teams, 2, sub, width), probes.reshape(teams, 2, sub, count))
    return result.reshape(2 * sub, count)


def solution(mesh):
    in_specs = (P("blk", None), P("blk", None))
    out_specs = P(("blk", "team"), None)
    return jax.shard_map(body, mesh=mesh, in_specs=in_specs, out_specs=out_specs, check_vma=False)
```

```python
import functools

import jax
import jax.numpy as jnp
from jax import lax
from jax.experimental import pallas as pl
from jax.experimental.pallas import tpu as pltpu
from jax.sharding import PartitionSpec as P

MESH = pl.DeviceIdType.MESH
CHUNKS = 4
LEAPS = 1
CORES = 2


def kernel(
    outer,
    inner,
    teams,
    points_hbm,
    probes_hbm,
    out_ref,
    layer_all,
    visitors,
    visitor_vals,
    cols_high,
    cols_low,
    vals_high,
    vals_low,
    layer_sq,
    terms,
    visitor_sq,
    second,
    sums,
    returned,
    partial,
    scattered,
    load_sem,
    visit_send,
    visit_recv,
    leap_send,
    ready,
    gift_send,
    gift_recv,
    row_send,
    plane_send,
    share_send,
    row_recv,
    back_send,
    back_recv,
    part_send,
    part_recv,
):
    sub, count = sums.shape[2:]
    width = layer_all.shape[-1] - count
    every = width + count
    half = outer // 2
    planes = teams // CORES
    wide = teams * sub
    step_rows = 2 * sub // CHUNKS
    scale = 2.0 / width
    block = lax.axis_index("blk")
    team = lax.axis_index("team")
    z = block // inner
    x = lax.rem(block, inner)
    plane = team // CORES
    core = lax.rem(team, CORES)
    left = z < half
    near = jnp.where(left, 1, -1)
    place = jnp.where(left, z, outer - 1 - z)

    def at(layer, column, member=None):
        target = {"blk": layer * inner + column}
        if member is not None:
            target["team"] = member
        return target

    def slot(layer):
        return jnp.where(layer < half, 2 * layer, 2 * (outer - 1 - layer) + 1)

    def inside(layer):
        return layer * (outer - 1 - layer) >= 0

    def remote(src, dst, send, recv, target):
        return pltpu.make_async_remote_copy(
            src_ref=src, dst_ref=dst, send_sem=send, recv_sem=recv, device_id=target, device_id_type=MESH
        )

    def wait_recv(ref, sem):
        pltpu.make_async_copy(ref, ref, sem).wait()

    def chunk(k):
        return (k * 2) // CHUNKS, pl.ds((k % (CHUNKS // 2)) * step_rows, step_rows)


    def same_side(layer, way):
        return (layer < half) if way == 1 else (layer >= half)

    def visit(layer, way, k, first, op):
        part, rows = chunk(k)
        dst = visitors.at[part, slot(layer), rows]

        op(remote(
            layer_all.at[part, x, team, rows, pl.ds(0, width)] if first else dst,
            dst,
            visit_send.at[layer, (way + 1) // 2, k],
            visit_recv.at[layer, k],
            at(z + way, x),
        ))

    def start(copy):
        copy.start()

    def wait_send(copy):
        copy.wait_send()

    last = CHUNKS - 1

    def rank(layer):
        return jnp.minimum(layer, outer - 1 - layer)

    def is_end(layer):
        return rank(layer) == 0

    def own_visits(way, k, op):
        first, final = (0, outer - 2) if way == 1 else (1, outer - 1)
        if k >= CHUNKS // 2:
            first, final = (0, half - 1) if way == 1 else (half, outer - 1)

        @pl.when((z - first) * (final - z) >= 0)
        def _():
            visit(z, way, k, True, op)

    def leaps(k, op):
        part, rows = chunk(k)

        @pl.when((place == 0) & (outer > 3))
        def _():
            op(remote(
                layer_all.at[part, x, team, rows, pl.ds(0, width)],
                visitors.at[part, slot(z), rows],
                leap_send.at[k],
                visit_recv.at[z, k],
                at(z + 2 * near, x),
            ))

    def goes_on(layer, way, k):
        low, high = (0, outer - 2) if way == 1 else (1, outer - 1)
        first, final = 0, outer - 1
        if k < CHUNKS // 2:
            room = (z - low) * (high - z)
        else:
            first, final = (0, half - 1) if way == 1 else (half, outer - 1)
            room = outer - 1 - layer - (z + way) if way == 1 else layer + (z + way) - (outer - 1)
        leapt = layer + z - 2 if way == 1 else 2 * outer - 4 - layer - z
        if k < LEAPS or outer < 4:
            leapt = 0
        return jnp.minimum(jnp.minimum((layer - first) * (final - layer), room), leapt) >= 0

    def wait_visit(layer, k):
        part, rows = chunk(k)
        wait_recv(visitors.at[part, slot(layer), rows], visit_recv.at[layer, k])

    def forward(distance, k):
        for way in (1, -1):
            layer = z - way * distance

            @pl.when(goes_on(layer, way, k))
            def _(way=way, layer=layer):
                wait_visit(layer, k)
                visit(layer, way, k, False, start)

    def asked(distance):
        return (place == 0) & (distance > 2) & (distance < outer - 1)

    def settle(layer, part):
        for k in range(part * CHUNKS // 2, (part + 1) * CHUNKS // 2):
            for way in (1, -1):
                ahead = way * (z - layer) > 0
                stays = ahead & jnp.logical_not(goes_on(layer, way, k))
                if part == 1:
                    stays = stays & (rank(layer) <= place)
                if k == 0:
                    stays = stays & jnp.logical_not(asked(way * (z - layer)))

                @pl.when(stays)
                def _(k=k):
                    wait_visit(layer, k)

    def gift(distance, op, ends=None):
        room = outer - 2 - 2 * place - distance
        if ends is not None:
            room = jnp.minimum(room, -place if ends else place - 1)

        @pl.when(room >= 0)
        def _():
            op(remote(
                layer_all.at[:, x, team, :, pl.ds(width, count)],
                visitor_vals.at[:, slot(z)],
                gift_send.at[distance],
                gift_recv.at[z],
                at(z + near * distance, x),
            ))

    def gift_afar(distance):
        if distance < outer - 1:
            @pl.when(place == 0)
            def _():
                wait_visit(z + near * distance, 0)
            gift(distance, start)


    def piece(column, member, k):
        begin, size = ((0, sub // 2), (sub // 2, sub // 2), (0, sub // 4), (sub // 4, 3 * sub // 4))[k]
        return layer_all.at[k // (CHUNKS // 2), column, member, pl.ds(begin, size)]

    def arrives(k, other):
        return k == CHUNKS - 1 or other == 0

    def member_of(other):
        return lax.rem(plane + other, planes) * CORES + core

    def across(step, k):
        return [
            remote(
                piece(x, member_of(other), k),
                piece(x, member_of(other), k),
                row_send.at[step - 1, k + other],
                row_recv.at[x, member_of(other), k],
                at(z, lax.rem(x + step, inner)),
            )
            for other in range(planes)
            if arrives(k, other)
        ]

    def along(step, k, other):
        column = lax.rem(x + step, inner)
        return remote(
            piece(column, team, k),
            piece(column, team, k),
            plane_send.at[step - 1, other - 1, k],
            row_recv.at[column, team, k],
            at(z, x, member_of(other)),
        )

    def share(step, k, other):
        column = lax.rem(x + step, inner)
        return remote(
            piece(column, member_of(other), k),
            piece(column, member_of(other), k),
            share_send.at[step - 1, other, k],
            row_recv.at[column, member_of(other), k],
            at(z, x, team + 1 - 2 * core),
        )

    def others(work):
        if inner == 2:
            work(1, 1 - x)
            return

        def one(step, carry):
            work(step, lax.rem(x + step, inner))
            return carry
        lax.fori_loop(1, inner, one, 0)

    def wait_piece(column, member, k):
        wait_recv(piece(column, member, k), row_recv.at[column, member, k])

    def take_across(k):
        def take(step, column):
            for other in range(planes):
                if arrives(k, other):
                    wait_piece(column, member_of(other), k)
                    if k < CHUNKS - 1:
                        for further in range(1, planes):
                            along(step, k, further).start()
                    share(step, k, other).start()
        others(take)

    def take_along(k):
        def take(step, column):
            for other in range(1, planes):
                wait_piece(column, member_of(other), k)
                share(step, k, other).start()
        others(take)

    def take_shared(k):
        def take(step, column):
            for other in range(planes):
                wait_piece(column, member_of(other) + 1 - 2 * core, k)
        others(take)


    def back(layer, part):
        return remote(
            sums.at[part, slot(layer)],
            returned.at[part, slot(z)],
            back_send.at[part, layer],
            back_recv.at[part, z],
            at(layer, x),
        )

    def visits_me(layer, part):
        if part == 0:
            return layer != z
        return (layer != z) & (rank(layer) <= place)

    def i_visit(layer, part):
        if part == 0:
            return layer != z
        return (layer != z) & (place <= rank(layer))

    peers = [
        (step, other, turn)
        for step in (*range(1, inner), 0)
        for other in (*range(1, planes), 0)
        for turn in range(CORES)
        if (step, other, turn) != (0, 0, 0)
    ]

    def scatter(peer):
        step, other, turn = peer
        column = lax.rem(x + step, inner)
        member = lax.rem(plane + other, planes) * CORES + lax.rem(core + turn, CORES)
        return remote(
            partial.at[column, member],
            scattered.at[x * teams + team],
            part_send.at[column * teams + member],
            part_recv.at[x * teams + team],
            at(z, column, member),
        )


    def two_terms(values):
        high = values.astype(jnp.bfloat16)
        return high, (values - high.astype(jnp.float32)).astype(jnp.bfloat16)

    def four_products(stacked, high, low, contract):
        rows = stacked.shape[0] // 2
        dot = functools.partial(
            lax.dot_general,
            dimension_numbers=(contract, ((), ())),
            preferred_element_type=jnp.float32,
        )
        by_high, by_low = dot(stacked, high), dot(stacked, low)
        return by_high[:rows] + (by_high[rows:] + by_low[:rows] + by_low[rows:])

    def prepare_columns(part, column):
        where = slice(part * wide, (part + 1) * wide)
        values = layer_all[part, column, :, :, 0:width].reshape(wide, width)
        total = jnp.sum(values * values, axis=1, keepdims=True)
        layer_sq[column, :, where] = jnp.broadcast_to(total, (wide, 128)).T[0:1, :]
        cols_high[column, where], cols_low[column, where] = two_terms(values)
        rest = layer_all[part, column, :, :, width:every].reshape(wide, count)
        vals_high[column, where], vals_low[column, where] = two_terms(rest)

    def prepare_rows(part, layer, values):
        where = pl.ds(pl.multiple_of(slot(layer) * sub, sub), sub)
        visitor_sq[part, where] = jnp.sum(values * values, axis=1, keepdims=True)
        high, low = two_terms(values)
        terms[part, 0, where, :] = high
        terms[part, 1, where, :] = low

    def pair(part, begin, size, column, fresh):
        rows = slice(begin * sub, (begin + size) * sub)
        cross = four_products(
            terms[part, :, rows, :].reshape(2 * size * sub, width),
            cols_high[column],
            cols_low[column],
            ((1,), (1,)),
        )
        arg = (visitor_sq[part, rows] + layer_sq[column] - 2.0 * cross) * scale
        value = jnp.exp(-jnp.maximum(arg, 0.0))
        second[part, rows, pl.ds(pl.multiple_of(column * wide, wide), wide)] = value[:, wide:]
        product = four_products(
            jnp.concatenate(two_terms(value), axis=0), vals_high[column], vals_low[column], ((1,), (0,))
        ).reshape(size, sub, count)
        kept = slice(begin, begin + size)
        sums[part, kept] = product if fresh else sums[part, kept] + product

    def outward(index):
        for layer in (index, outer - 1 - index):
            wait_recv(visitor_vals.at[:, slot(layer)], gift_recv.at[layer])
        rows = slice(2 * index * sub, 2 * (index + 1) * sub)
        value = jnp.concatenate([second[0, rows, :], second[1, rows, :]], axis=0).T
        rest = visitor_vals[:, 2 * index : 2 * (index + 1)].reshape(4 * sub, count)
        high, low = two_terms(rest)
        product = four_products(jnp.concatenate(two_terms(value), axis=0), high, low, ((1,), (0,)))
        product = product.reshape(inner, teams, sub, count)
        partial[...] = product if index == 0 else partial[...] + product


    loads = [
        pltpu.make_async_copy(
            source.at[:, part], layer_all.at[part, x, :, :, pl.ds(begin, extent)], load_sem.at[part, which]
        )
        for part in range(2)
        for which, (source, begin, extent) in enumerate(((points_hbm, 0, width), (probes_hbm, width, count)))
    ]
    barrier = pltpu.get_barrier_semaphore()

    def greet(target):
        pl.semaphore_signal(barrier, inc=1, device_id=target, device_id_type=MESH)

    for way in (1, -1):
        @pl.when(inside(z + way))
        def _(way=way):
            greet(at(z + way, x))
    for step in range(1, inner):
        greet(at(z, lax.rem(x + step, inner)))
    for other in range(1, planes):
        greet(at(z, x, member_of(other)))
    greet(at(z, x, team + 1 - 2 * core))
    for load in loads:
        load.start()
    for load in loads:
        load.wait()
    pl.semaphore_wait(barrier, jnp.where(is_end(z), 1, 2) + inner - 1 + planes)

    if outer > 3:
        @pl.when(place == 1)
        def _():
            pl.semaphore_signal(ready, inc=1, device_id=at(z - near, x), device_id_type=MESH)


    for k in range(CHUNKS):
        if k < CHUNKS // 2:
            for way in (1, -1):
                own_visits(way, k, start)
        for step in range(1, inner):
            for copy in across(step, k):
                copy.start()

    for part in range(2):
        prepare_columns(part, x)
        prepare_rows(part, z, layer_all[part, x, team, :, 0:width])

    if outer > 3:
        @pl.when(place == 0)
        def _():
            pl.semaphore_wait(ready, 1)
    for k in range(LEAPS, CHUNKS):
        leaps(k, start)
    for k in range(CHUNKS // 2, CHUNKS):
        for way in (1, -1):
            @pl.when(place == 0)
            def _(way=way, k=k):
                own_visits(way, k, start)
    gift(1, start)
    gift(2, start, True)

    def forward_far(k):
        if outer > 3:
            forward(2, k)

    def own_second():
        @pl.when(place > 0)
        def _():
            for k in range(CHUNKS // 2, CHUNKS):
                for way in (1, -1):
                    own_visits(way, k, start)

    for k in range(last):
        forward(1, k)
        take_across(k)
        if k == 0:
            own_second()
    forward(1, last)

    forward_far(1)
    forward_far(0)
    gift(2, start, False)
    forward_far(2)
    take_along(0)
    forward_far(last)
    for distance in range(3, outer - 1):
        for k in range(CHUNKS):
            forward(distance, k)
        gift_afar(distance)

    def meet_first():
        for step in range(1, outer):
            layer = lax.rem(z + step, outer)
            settle(layer, 0)
            prepare_rows(0, layer, visitors[0, slot(layer)])
        pair(0, 0, outer, x, True)

    def meet(index):
        for layer in (index, outer - 1 - index):
            settle(layer, 1)

            @pl.when(visits_me(layer, 1))
            def _(layer=layer):
                prepare_rows(1, layer, visitors[1, slot(layer)])
        pair(1, 2 * index, 2, x, True)

    @pl.when(place > 0)
    def _():
        meet_first()
    take_along(1)
    take_along(2)
    take_across(last)
    @pl.when(place == 0)
    def _():
        meet_first()
    take_shared(0)
    take_shared(1)
    others(lambda step, column: prepare_columns(0, column))

    take_shared(2)
    take_shared(last)
    others(lambda step, column: prepare_columns(1, column))

    others(lambda step, column: pair(0, 0, outer, column, False))
    for distance in range(outer - 1, 0, -1):
        for way in (1, -1):
            @pl.when(inside(z + way * distance))
            def _(layer=z + way * distance):
                back(layer, 0).start()

    meet(0)
    for index in range(half):
        def finish(index=index):
            if index > 0:
                meet(index)
            others(lambda step, column: pair(1, 2 * index, 2, column, False))
            for layer in (index, outer - 1 - index):
                @pl.when(layer != z)
                def _(layer=layer):
                    back(layer, 1).start()

        if index == 0:
            finish()
        else:
            pl.when(place >= index)(finish)
        if index < half - 1:
            @pl.when(place > index)
            def _(index=index):
                outward(index)

            @pl.when(place == index + 1)
            def _():
                for peer in peers:
                    scatter(peer).start()


    for k in range(LEAPS, CHUNKS):
        leaps(k, wait_send)
    for way in (1, -1):
        for k in range(CHUNKS):
            own_visits(way, k, wait_send)
            for distance in range(1, outer - 1):
                layer = z - way * distance

                @pl.when(goes_on(layer, way, k))
                def _(way=way, k=k, layer=layer):
                    visit(layer, way, k, False, wait_send)
    for distance in range(1, outer - 1):
        gift(distance, wait_send)

    def sent(step, column):
        for k in range(CHUNKS):
            for copy in across(step, k):
                copy.wait_send()
            for other in range(planes):
                if other > 0 and k < CHUNKS - 1:
                    along(step, k, other).wait_send()
                share(step, k, other).wait_send()
    others(sent)


    mine = slot(z)
    for part in range(2):
        result = sums[part, mine]
        if part == 0:
            for step in range(1, outer):
                layer = lax.rem(z + step, outer)
                wait_recv(returned.at[0, slot(layer)], back_recv.at[0, layer])
                result = result + returned[0, slot(layer)]
            out_ref[0] = result
        else:
            out_ref[1] = result
            for step in range(1, outer):
                layer = lax.rem(z + step, outer)

                @pl.when(i_visit(layer, 1))
                def _(layer=layer):
                    wait_recv(returned.at[1, slot(layer)], back_recv.at[1, layer])
                    out_ref[1] = out_ref[1] + returned[1, slot(layer)]

            @pl.when(place > 0)
            def _():
                own = x * teams + team
                total = out_ref[1] + partial[x, team]
                for step in range(1, inner * teams):
                    index = lax.rem(own + step, inner * teams)
                    wait_recv(scattered.at[index], part_recv.at[index])
                    total = total + scattered[index]
                out_ref[1] = total
                for peer in peers:
                    scatter(peer).wait_send()
    for step in range(1, outer):
        layer = lax.rem(z + step, outer)
        for part in range(2):
            @pl.when(visits_me(layer, part))
            def _(layer=layer, part=part):
                back(layer, part).wait_send()


def body(points, probes):
    rows, width = points.shape
    count = probes.shape[1]
    blocks, teams = lax.axis_size("blk"), lax.axis_size("team")
    inner = 1 << ((blocks.bit_length() - 1) // 2)
    outer = blocks // inner
    sub = rows // teams // 2
    every = width + count
    f32, bf16 = jnp.float32, jnp.bfloat16
    dma = pltpu.SemaphoreType.DMA
    planes = teams // CORES
    result = pl.pallas_call(
        functools.partial(kernel, outer, inner, teams),
        out_shape=jax.ShapeDtypeStruct((2, sub, count), f32),
        in_specs=[pl.BlockSpec(memory_space=pl.ANY)] * 2,
        out_specs=pl.BlockSpec(memory_space=pltpu.VMEM),
        scratch_shapes=[
            pltpu.VMEM((2, inner, teams, sub, every), f32),
            pltpu.VMEM((2, outer, sub, width), f32),
            pltpu.VMEM((2, outer, sub, count), f32),
            pltpu.VMEM((inner, 2 * teams * sub, width), bf16),
            pltpu.VMEM((inner, 2 * teams * sub, width), bf16),
            pltpu.VMEM((inner, 2 * teams * sub, count), bf16),
            pltpu.VMEM((inner, 2 * teams * sub, count), bf16),
            pltpu.VMEM((inner, 1, 2 * teams * sub), f32),
            pltpu.VMEM((2, 2, outer * sub, width), bf16),
            pltpu.VMEM((2, outer * sub, 1), f32),
            pltpu.VMEM((2, outer * sub, inner * teams * sub), f32),
            pltpu.VMEM((2, outer, sub, count), f32),
            pltpu.VMEM((2, outer, sub, count), f32),
            pltpu.VMEM((inner, teams, sub, count), f32),
            pltpu.VMEM((inner * teams, sub, count), f32),
            dma((2, 2)),
            dma((outer, 2, CHUNKS)),
            dma((outer, CHUNKS)),
            dma((CHUNKS,)),
            pltpu.SemaphoreType.REGULAR,
            dma((outer,)),
            dma((outer,)),
            dma((inner - 1, CHUNKS + planes - 1)),
            dma((inner - 1, planes - 1, CHUNKS)),
            dma((inner - 1, planes, CHUNKS)),
            dma((inner, teams, CHUNKS)),
            dma((2, outer)),
            dma((2, outer)),
            dma((inner * teams,)),
            dma((inner * teams,)),
        ],
        compiler_params=pltpu.CompilerParams(
            collective_id=0, has_side_effects=True, vmem_limit_bytes=55100 * 2**10
        ),
    )(points.reshape(teams, 2, sub, width), probes.reshape(teams, 2, sub, count))
    return result.reshape(2 * sub, count)


def solution(mesh):
    in_specs = (P("blk", None), P("blk", None))
    out_specs = P(("blk", "team"), None)
    return jax.shard_map(body, mesh=mesh, in_specs=in_specs, out_specs=out_specs, check_vma=False)
```
